32 devices in a mesh: dp: 8 (over y, x, core), mp: 4 (over z).
Axes of the slice: x: 2, y: 2, z: 4, core: 2. Of those that a mesh axis runs over, the one named last changes fastest.
Arguments:
- tokens: bfloat16 [8192, 5120], P('dp'), may hold values from -6 to 6
- norm_gain: bfloat16 [5120], replicated, may hold values from 0.099609375 to 1.8984375
- w_query: bfloat16 [5120, 5120], P('dp', 'mp'), may hold values from -0.078125 to 0.078125
- b_query: bfloat16 [5120], P('mp'), may hold values from -3 to 3
- keyvalue_weight: bfloat16 [5120, 2, 1024], P('dp', None, 'mp'), may hold values from -0.078125 to 0.078125
- b_keyval: bfloat16 [2, 1024], P(None, 'mp'), may hold values from -3 to 3
- w_out: bfloat16 [5120, 5120], P('mp', 'dp'), may hold values from -0.5 to 0.5
- kv_pool: bfloat16 [2, 512, 64, 1024], P(None, 'dp', None, 'mp'), may hold values from -64 to 64
- page_owner: int32 [8, 16], replicated, may hold values from 0 to 7, as said below
- page_index: int32 [8, 16], replicated, may hold values from 0 to 63
- prefix_pages: int32 [8], replicated, may hold values from 10 to 16, as said below
- prompt_device: int32 [8], replicated, may hold values from 0 to 7, each once
Outputs:
- attn_out: bfloat16 [8192, 5120], P('dp', 'mp')
The draws below stay inside these ranges and needn't reach their ends.
Inputs may be any that keep to these rules, and one draw needn't show every extreme that they name: `page_owner`: slots at or beyond a prompt's prefix_pages are unused. Of one prompt's used slots at most 2 name the same owner, and some prompt has exactly 2 used slots with one owner. `prefix_pages`: some prompt has 16 used slots.
All inputs are finite; a program needn't handle non-finite values.
Results may differ from the reference program's by a relative error of at most 0.014.
The reference program's roundings to bfloat16 on the way count: a program that leaves them out, or rounds other values in their place, can miss the bound.
Values may be sent and summed in bfloat16 or wider, within the bound.
A program may use at most 192 MiB of HBM per device.

```python
import jax
import jax.numpy as jnp
from jax import lax

D = 5120
H = 40
KVH = 8
HD = 128
SUFFIX = 1024
PAGE = 64
MAXP = 16
CAP = 2
POOL = 64
TOKENS = 8192
N_DP = 8
N_MP = 4


def page_plan(key):
    base = jax.random.fold_in(key, 7)
    key_len, key_top, key_rating, key_frequent, key_index = jax.random.split(base, 5)
    lengths = jax.random.randint(key_len, (N_DP,), MAXP - 3 * MAXP // 8, MAXP + 1)
    longest = jax.random.randint(key_top, (), 0, N_DP)
    lengths = jnp.where(jnp.arange(N_DP) == longest, MAXP, lengths).astype(jnp.int32)
    frequent_ranking = jax.random.permutation(key_frequent, N_DP)
    frequent_count = max(1, N_DP // 4)
    score_extra = jnp.where(frequent_ranking < frequent_count, 512, 0)
    logit_scores = jax.random.randint(key_rating, (N_DP, N_DP), 0, 1024) - score_extra[None, :]
    distinct = logit_scores * N_DP + jnp.arange(N_DP)[None, :]
    owner_list = jnp.argsort(distinct, axis=1, stable=True)
    slot_run = jnp.broadcast_to((jnp.arange(MAXP) // CAP)[None, :], (N_DP, MAXP))
    owners = jnp.take_along_axis(owner_list, slot_run, axis=1).astype(jnp.int32)
    indices = jax.random.randint(key_index, (N_DP, MAXP), 0, POOL).astype(jnp.int32)
    return (owners, indices, lengths)


def draw_page_owner(key, part):
    return page_plan(key)[0]


def draw_page_index(key, part):
    return page_plan(key)[1]


def draw_prefix_pages(key, part):
    return page_plan(key)[2]


def draw_kv_pool(key, part):
    key_main = jax.random.fold_in(jax.random.fold_in(key, 11), 0)
    shape = (2, N_DP * POOL, PAGE, KVH * HD)
    values = jnp.clip(jax.random.normal(key_main, shape, jnp.float32), -6.0, 6.0)
    return values.astype(jnp.bfloat16)


def block_scale(key, extent, cuts, smallest, top_value):
    def one(position, shards_of):
        heights = jax.random.uniform(jax.random.fold_in(jax.random.fold_in(key, 6), position), (shards_of,), jnp.float32, smallest / len(cuts), top_value / len(cuts))
        return jnp.repeat(jnp.exp(heights), extent[position] // shards_of).reshape((-1,) + (1,) * (len(extent) - position - 1))

    loudness = one(*cuts[0])
    for cut in cuts[1:]:
        loudness = loudness * one(*cut)
    return loudness


def bell_draw(rng, extent, scale, bound, cuts=(), held_as=jnp.bfloat16):
    drawn = scale * jax.random.normal(rng, extent, jnp.float32)
    if cuts:
        drawn = drawn * block_scale(rng, extent, cuts, -0.22, 0.18)
    return jnp.clip(drawn, -bound, bound).astype(held_as)


def setup_inputs(seed: int = 0) -> dict:
    splits = jax.random.split(jax.random.key(seed), 13)
    return {
        "tokens": bell_draw(splits[0], (TOKENS, D), 1.0, 6.0, ((0, 8),)),
        "norm_gain": jnp.clip(1.0 + 0.18 * jax.random.normal(splits[1], (D,), jnp.float32), 0.099609375, 1.8984375).astype(jnp.bfloat16),
        "w_query": bell_draw(splits[2], (D, H * HD), D ** -0.5, 0.078125, ((0, 8), (1, 4))),
        "b_query": bell_draw(splits[3], (H * HD,), 0.5, 3.0, ((0, 4),)),
        "keyvalue_weight": bell_draw(splits[4], (D, 2, KVH * HD), D ** -0.5, 0.078125, ((0, 8), (2, 4))),
        "b_keyval": bell_draw(splits[5], (2, KVH * HD), 0.5, 3.0, ((1, 4),)),
        "w_out": bell_draw(splits[6], (H * HD, D), HD ** -0.5, 0.5, ((0, 4), (1, 8))),
        "kv_pool": draw_kv_pool(jax.random.fold_in(splits[12], 71), 0),
        "page_owner": draw_page_owner(jax.random.fold_in(splits[12], 71), 0),
        "page_index": draw_page_index(jax.random.fold_in(splits[12], 71), 0),
        "prefix_pages": draw_prefix_pages(jax.random.fold_in(splits[12], 71), 0),
        "prompt_device": jax.random.permutation(splits[11], N_DP).astype(jnp.int32),
    }


rope_theta = 1000000.0
norm_eps = 1e-06
masked_score = -1e+30

def rms_normed(rows, norm_gain):
    values = rows.astype(jnp.float32)
    inverse = lax.rsqrt(lax.optimization_barrier(jnp.mean(values * values, axis=-1, keepdims=True)) + norm_eps)
    return (values * inverse * norm_gain.astype(jnp.float32)).astype(jnp.bfloat16)

def rotary(values, positions):
    half_dim = values.shape[-1] // 2
    frequency = rope_theta ** (-jnp.arange(half_dim, dtype=jnp.float32) * 2.0 / values.shape[-1])
    angles = positions.astype(jnp.float32)[:, None] * frequency[None, :]
    cosine = jnp.cos(angles)[:, None, :]
    sine_part = jnp.sin(angles)[:, None, :]
    front_half = values[..., :half_dim]
    back_half = values[..., half_dim:]
    return jnp.concatenate([front_half * cosine - back_half * sine_part, back_half * cosine + front_half * sine_part], axis=-1)

def head_attention(query, keys, values, allowed):
    logit_scores = jnp.einsum('sgd,nd->gsn', query.astype(jnp.float32), keys.astype(jnp.float32)) * HD ** (-0.5)
    logit_scores = jnp.where(allowed[None], logit_scores, masked_score)
    top = lax.optimization_barrier(jnp.max(logit_scores, axis=-1, keepdims=True))
    raised = jnp.exp(logit_scores - top)
    weights = (raised / lax.optimization_barrier(jnp.sum(raised, axis=-1, keepdims=True))).astype(jnp.bfloat16)
    return jnp.einsum('gsn,nd->sgd', weights.astype(jnp.float32), values.astype(jnp.float32)).astype(jnp.bfloat16)

def reference(tokens, norm_gain, w_query, b_query, keyvalue_weight, b_keyval, w_out, kv_pool, page_owner, page_index, prefix_pages, prompt_device):
    slot_prompt = jnp.zeros((N_DP,), jnp.int32).at[prompt_device].set(jnp.arange(N_DP, dtype=jnp.int32))
    token_blocks = tokens.reshape(N_DP, SUFFIX, D)
    flat_keyval = keyvalue_weight.reshape(D, 2 * KVH * HD)

    def one_group(item):
        rows, prompt = item
        normed = rms_normed(rows, norm_gain)
        query = jnp.dot(normed, w_query, preferred_element_type=jnp.float32) + b_query.astype(jnp.float32)
        keyval = jnp.dot(normed, flat_keyval, preferred_element_type=jnp.float32) + b_keyval.reshape(2 * KVH * HD).astype(jnp.float32)
        length = prefix_pages[prompt]
        positions = length * PAGE + jnp.arange(SUFFIX, dtype=jnp.int32)
        rotated = rotary(query.reshape(SUFFIX, H, HD), positions).astype(jnp.bfloat16)
        new_keys = rotary(keyval[:, :KVH * HD].reshape(SUFFIX, KVH, HD), positions).astype(jnp.bfloat16)
        new_values = keyval[:, KVH * HD:].reshape(SUFFIX, KVH, HD).astype(jnp.bfloat16)
        flat_pages = (page_owner[prompt] * POOL + page_index[prompt]).astype(jnp.int32)
        cached = jnp.take(kv_pool, flat_pages, axis=1).reshape(2, MAXP * PAGE, KVH, HD)
        keys = jnp.concatenate([cached[0], new_keys], axis=0)
        values = jnp.concatenate([cached[1], new_values], axis=0)
        page_live = jnp.arange(MAXP * PAGE, dtype=jnp.int32) < length * PAGE
        token_ids = jnp.arange(SUFFIX, dtype=jnp.int32)
        causal = token_ids[None, :] <= token_ids[:, None]
        allowed = jnp.concatenate([jnp.broadcast_to(page_live[None, :], (SUFFIX, MAXP * PAGE)), causal], axis=1)
        grouped = rotated.reshape(SUFFIX, KVH, H // KVH, HD).transpose(1, 0, 2, 3)
        heads_out = lax.map(lambda part: head_attention(part[0], part[1], part[2], allowed), (grouped, keys.transpose(1, 0, 2), values.transpose(1, 0, 2)))
        attended = heads_out.transpose(1, 0, 2, 3).reshape(SUFFIX, H * HD)
        per_shard = attended.reshape(SUFFIX, N_MP, H * HD // N_MP)
        out_rows = w_out.reshape(N_MP, H * HD // N_MP, D)
        total = jnp.zeros((SUFFIX, D), jnp.float32)
        for shard in range(N_MP):
            term = jnp.dot(per_shard[:, shard], out_rows[shard], preferred_element_type=jnp.float32)
            total = total + lax.optimization_barrier(term.astype(jnp.bfloat16)).astype(jnp.float32)
        return total.astype(jnp.bfloat16)
    result = lax.map(one_group, (token_blocks, slot_prompt))
    return result.reshape(N_DP * SUFFIX, D)
```

```python
import functools
import math

import jax
import jax.numpy as jnp
from jax import lax
from jax.experimental import pallas as pl
from jax.experimental.pallas import tpu as pltpu
from jax.sharding import PartitionSpec as P


HD = 128
CAP = 2
ROW_PARTS = 2


rope_theta = 1000000.0
norm_eps = 1e-06
masked_score = -1e30


def rms_normed(rows, norm_gain):
    values = rows.astype(jnp.float32)
    inverse = lax.rsqrt(jnp.mean(values * values, axis=-1, keepdims=True) + norm_eps)
    return (values * inverse * norm_gain.astype(jnp.float32)).astype(jnp.bfloat16)


def rotary_tables(positions):
    half_dim = HD // 2
    frequency = rope_theta ** (-jnp.arange(half_dim, dtype=jnp.float32) * 2.0 / HD)
    angles = positions.astype(jnp.float32)[:, None] * frequency[None, :]
    cosine = jnp.cos(angles)
    sine = jnp.sin(angles)
    return (
        jnp.concatenate([cosine, cosine], axis=-1),
        jnp.concatenate([-sine, sine], axis=-1),
    )


def attention_kernel(block, prev_len, *refs):
    q_ref, k_ref, v_ref, cos_ref, sin_ref, bias_ref, kp_ref, vp_ref = refs[:8]
    refs = refs[8:]
    if prev_len:
        k_prev_ref, v_prev_ref = refs[:2]
        refs = refs[2:]
    o_ref, k_out, v_out = refs
    cosine = cos_ref[...]
    sine = sin_ref[...]

    def rotate(x):
        return (x * cosine + pltpu.roll(x, HD // 2, 1) * sine).astype(jnp.bfloat16)

    @pl.when(pl.program_id(0) == 0)
    def _():
        k_out[...] = rotate(k_ref[...])
        v_out[...] = v_ref[...].astype(jnp.bfloat16)

    query = rotate(q_ref[...])
    factor = HD ** (-0.5) * math.log2(math.e)
    rows = query.shape[0]
    ids = lax.broadcasted_iota(jnp.int32, (block, block), 0)
    keys_id = lax.broadcasted_iota(jnp.int32, (block, block), 1)

    def scores(q, k):
        return lax.dot_general(q, k, (((1,), (1,)), ((), ())), preferred_element_type=jnp.float32)

    for begin in range(0, rows, block):
        q = query[begin : begin + block]
        parts = [(scores(q, kp_ref[0]) + bias_ref[...], vp_ref[0])]
        if prev_len:
            parts.append((scores(q, k_prev_ref[...]), v_prev_ref[...]))
        if begin:
            parts.append((scores(q, k_out[0:begin, :]), v_out[0:begin, :]))
        diagonal = scores(q, k_out[begin : begin + block, :])
        diagonal = jnp.where(keys_id <= ids, diagonal, masked_score)
        parts.append((diagonal, v_out[begin : begin + block, :]))
        top = functools.reduce(
            jnp.maximum, [jnp.max(s, axis=-1, keepdims=True) for s, _ in parts]
        )
        total = None
        out = None
        for s, v in parts:
            raised = jnp.exp2((s - top) * factor)
            row_sum = jnp.sum(raised, axis=-1, keepdims=True)
            term = jnp.dot(raised.astype(jnp.bfloat16), v, preferred_element_type=jnp.float32)
            total = row_sum if total is None else total + row_sum
            out = term if out is None else out + term
        o_ref[begin : begin + block, :] = (out / total).astype(jnp.bfloat16)


def attention(group, qkv, cosine, sine, bias, arrived, prev, per_group):
    rows = qkv.shape[0]
    cached_len = arrived.shape[1]
    block = math.gcd(256, rows)
    const = lambda shape, index: pl.BlockSpec(shape, lambda h: index)
    in_specs = [
        pl.BlockSpec((rows, HD), lambda h: (0, h)),
        const((rows, HD), (0, per_group)),
        const((rows, HD), (0, per_group + 1)),
        const((rows, HD), (0, 0)),
        const((rows, HD), (0, 0)),
        const((1, cached_len), (0, 0)),
        const((1, cached_len, HD), (0, 0, group)),
        const((1, cached_len, HD), (1, 0, group)),
    ]
    operands = [qkv, qkv, qkv, cosine, sine, bias, arrived, arrived]
    prev_len = 0
    if prev is not None:
        prev_len = prev[0].shape[0]
        in_specs += [const((prev_len, HD), (0, 0))] * 2
        operands += list(prev)
    keys = cached_len + prev_len + rows
    return pl.pallas_call(
        functools.partial(attention_kernel, block, prev_len),
        grid=(per_group,),
        in_specs=in_specs,
        out_specs=[
            pl.BlockSpec((rows, HD), lambda h: (0, h)),
            const((rows, HD), (0, 0)),
            const((rows, HD), (0, 0)),
        ],
        out_shape=[
            jax.ShapeDtypeStruct((rows, per_group * HD), jnp.bfloat16),
            jax.ShapeDtypeStruct((rows, HD), jnp.bfloat16),
            jax.ShapeDtypeStruct((rows, HD), jnp.bfloat16),
        ],
        compiler_params=pltpu.CompilerParams(
            dimension_semantics=("arbitrary",), vmem_limit_bytes=40 * 1024 * 1024
        ),
        cost_estimate=pl.CostEstimate(
            flops=8 * per_group * rows * keys * HD,
            bytes_accessed=6 * rows * (per_group + 2) * HD,
            transcendentals=per_group * rows * keys,
        ),
    )(*operands)


def exchange(x, axis, split_axis, concat_axis):
    size = lax.axis_size(axis)
    me = lax.axis_index(axis)
    width = x.shape[split_axis] // size
    span = x.shape[concat_axis]
    shape = list(x.shape)
    shape[split_axis] = width
    shape[concat_axis] = span * size
    result = jnp.zeros(shape, x.dtype)
    for s in range(size):
        target = lax.rem(me + s, size)
        source = lax.rem(me - s + size, size)
        piece = lax.dynamic_slice_in_dim(x, target * width, width, split_axis)
        if s:
            piece = lax.ppermute(piece, axis, [(i, (i + s) % size) for i in range(size)])
        result = lax.dynamic_update_slice_in_dim(result, piece, source * span, concat_axis)
    return result


def shards(*arguments):
    kv_local = arguments[4].shape[2] // HD
    if square_mesh() and kv_local == 2:
        return fused_layer(*arguments)
    return layer(*arguments)


def square_mesh():
    return lax.axis_size("dp") == 8 and lax.axis_size("mp") == 4


def layer(
    tokens,
    norm_gain,
    w_query,
    b_query,
    keyvalue_weight,
    b_keyval,
    w_out,
    kv_pool,
    page_owner,
    page_index,
    prefix_pages,
    prompt_device,
):
    groups = lax.axis_size("dp")
    planes = lax.axis_size("mp")
    my_group = lax.axis_index("dp")
    my_plane = lax.axis_index("mp")
    seq_rows = tokens.shape[0]
    width_kv = keyvalue_weight.shape[2]
    kv_local = width_kv // HD
    heads_local = w_query.shape[1] // HD
    per_group = heads_local // kv_local
    page_len = kv_pool.shape[2]
    max_pages = page_owner.shape[1]
    group_ids = jnp.arange(groups, dtype=jnp.int32)

    width_q = per_group * HD
    gathered = []
    biases = []
    for g in range(kv_local):
        piece = jnp.concatenate(
            [
                w_query[:, g * width_q : (g + 1) * width_q],
                keyvalue_weight[:, 0, g * HD : (g + 1) * HD],
                keyvalue_weight[:, 1, g * HD : (g + 1) * HD],
            ],
            axis=1,
        )
        gathered.append(lax.all_gather(piece, "dp", axis=0, tiled=True))
        biases.append(
            jnp.concatenate(
                [
                    b_query[g * width_q : (g + 1) * width_q],
                    b_keyval[0, g * HD : (g + 1) * HD],
                    b_keyval[1, g * HD : (g + 1) * HD],
                ]
            ).astype(jnp.float32)
        )

    slot_prompt = jnp.sum(
        jnp.where(prompt_device[None, :] == group_ids[:, None], group_ids[None, :], 0), axis=1
    )
    owners_all = jnp.take(page_owner, slot_prompt, axis=0)
    index_all = jnp.take(page_index, slot_prompt, axis=0)
    length_all = jnp.take(prefix_pages, slot_prompt, axis=0)
    slot_ids = jnp.arange(max_pages, dtype=jnp.int32)
    places = jnp.arange(CAP, dtype=jnp.int32)
    used = slot_ids[None, :] < length_all[:, None]
    mine = used & (owners_all == my_group)
    rank = jnp.cumsum(mine.astype(jnp.int32), axis=1) - 1
    chosen = mine[:, None, :] & (rank[:, None, :] == places[None, :, None])
    send_index = jnp.sum(jnp.where(chosen, index_all[:, None, :], 0), axis=2)
    outgoing = jnp.take(kv_pool, send_index.reshape(-1), axis=1).reshape(
        2, groups, CAP, page_len, width_kv
    )
    arrived = lax.all_to_all(outgoing, "dp", split_axis=1, concat_axis=1, tiled=True)
    my_owners = jnp.take(owners_all, my_group, axis=0)
    my_length = jnp.take(length_all, my_group, axis=0)
    my_used = slot_ids < my_length
    counts = jnp.sum(
        ((my_owners[None, :] == group_ids[:, None]) & my_used[None, :]).astype(jnp.int32), axis=1
    )
    page_live = (places[None, :] < counts[:, None]).reshape(-1)
    cached_len = page_live.shape[0] * page_len
    arrived = arrived.reshape(2, cached_len, width_kv)
    bias = jnp.where(jnp.repeat(page_live, page_len), 0.0, masked_score).astype(jnp.float32)[None]

    normed = rms_normed(tokens, norm_gain)
    arrived, w_out = lax.optimization_barrier((arrived, w_out))
    out_rows = exchange(w_out, "dp", 0, 1)
    out_rows = exchange(out_rows, "mp", 1, 0)
    out_weight = lax.all_gather(out_rows, "dp", axis=0, tiled=True)
    out_cols = out_weight.shape[1]
    out_weight = out_weight.reshape(groups, planes, -1, out_cols)
    cosine, sine = rotary_tables(
        my_length * page_len + jnp.arange(seq_rows, dtype=jnp.int32)
    )
    part = seq_rows // ROW_PARTS
    held = [[[] for _ in range(ROW_PARTS)] for _ in range(planes)]
    for g in range(kv_local):
        prev = None
        for r in range(ROW_PARTS):
            rows = slice(r * part, (r + 1) * part)
            qkv = (
                jnp.dot(normed[rows], gathered[g], preferred_element_type=jnp.float32)
                + biases[g]
            )
            attended, keys, values = attention(
                g, qkv, cosine[rows], sine[rows], bias, arrived, prev, per_group
            )
            if prev is None:
                prev = (keys, values)
            else:
                prev = (
                    jnp.concatenate([prev[0], keys], axis=0),
                    jnp.concatenate([prev[1], values], axis=0),
                )
            held[0][r].append(attended)
            for s in range(1, planes):
                high = 1 << (s.bit_length() - 1)
                low = s - high
                _, moved, step = ("relay", held[high][r][g], low) if low else ("send", attended, s)
                held[s][r].append(lax.ppermute(moved, "mp", [(i, i ^ step) for i in range(planes)]))
    weights = []
    for s in range(planes):
        source = my_plane ^ s
        rows_of = lax.dynamic_index_in_dim(out_weight, source, axis=1, keepdims=False)
        weights.append(rows_of.reshape(-1, out_cols))
    outputs = []
    for r in range(ROW_PARTS):
        total = None
        for s in range(planes):
            head_partial = None
            for g in range(kv_local):
                term = jnp.dot(
                    held[s][r][g],
                    weights[s][g * width_q : (g + 1) * width_q],
                    preferred_element_type=jnp.float32,
                )
                head_partial = term if head_partial is None else term + head_partial
            head_partial = head_partial.astype(jnp.bfloat16).astype(jnp.float32)
            total = head_partial if total is None else total + head_partial
        outputs.append(total.astype(jnp.bfloat16))
    return jnp.concatenate(outputs, axis=0)


MESH = pl.DeviceIdType.MESH
BLOCK = 256
TILE = 2 * HD
X, Y, FAR, OWN, OX, OY, OFAR = range(7)


def fused_kernel(
    tokens, w_query, w_keyval, w_out, outgoing, gain, bias, mask, cosine, sine,
    out, relay,
    normed, wqkv, wout, cache, keys, values, query, att, att_in, part_in,
    token_sem, own_sem, send_sem, recv_sem, page_send, page_recv, page_own,
    z_send, z_recv, part_send, part_recv, move_send, move_recv, out_sem,
):
    div, rem = lax.div, lax.rem
    groups = lax.axis_size("dp")
    planes = lax.axis_size("mp")
    d = lax.axis_index("dp")
    m = lax.axis_index("mp")
    rows = tokens.shape[0]
    half_rows = rows // 2
    blocks = rows // BLOCK
    depth = w_query.shape[0]
    q_width = w_query.shape[1]
    tiles = q_width // TILE
    kv_chunks = w_keyval.shape[1] // TILE
    per_group = q_width // HD // kv_chunks
    chunks = kv_chunks + tiles
    out_depth, out_cols = w_out.shape
    out_parts = 2
    part_depth = out_depth // out_parts

    core = rem(d, 2)
    x_bit = rem(div(d, 2), 2)
    y_bit = rem(div(d, 4), 2)
    core_n = d + 1 - 2 * core
    x_n = d + 2 - 4 * x_bit
    y_n = d + 4 - 8 * y_bit
    far = x_n + y_n - d
    far_src = x_n + core * (y_n - x_n)
    far_dst = y_n + core * (x_n - y_n)

    def piece(k, owner):
        if isinstance(k, int) and k >= chunks:
            return wout.at[owner, pl.ds((k - chunks) * part_depth, part_depth), :]
        return wqkv.at[
            pl.ds(pl.multiple_of(owner * depth, depth), depth),
            pl.ds(pl.multiple_of(k * TILE, TILE), TILE),
        ]

    routes = {
        X: (d, x_n),
        Y: (d, y_n),
        FAR: (far_src, far_dst),
        OWN: (d, core_n),
        OX: (x_n, core_n),
        OY: (y_n, core_n),
        OFAR: (far, core_n),
    }

    def hop(kind, k):
        owner, target = routes[kind]
        region = piece(k, owner)
        return pltpu.make_async_remote_copy(
            src_ref=region,
            dst_ref=region,
            send_sem=send_sem.at[kind, k],
            recv_sem=recv_sem.at[kind, k],
            device_id=(target, m),
            device_id_type=MESH,
        )

    def issue(k):
        for kind in (X, Y, OWN):
            hop(kind, k).start()

    def forward(k):
        hop(X, k).wait_recv()
        hop(Y, k).wait_recv()
        for kind in (FAR, OX, OY):
            hop(kind, k).start()

    def complete(k):
        hop(FAR, k).wait_recv()
        hop(OFAR, k).start()
        for kind in (OWN, OX, OY, OFAR):
            hop(kind, k).wait_recv()

    barrier = pltpu.get_barrier_semaphore()
    for s in range(1, groups):
        pl.semaphore_signal(
            barrier, inc=1, device_id=(rem(d + s, groups), m), device_id_type=MESH
        )
    for s in range(1, planes):
        pl.semaphore_signal(
            barrier, inc=1, device_id=(d, rem(m + s, planes)), device_id_type=MESH
        )

    def own_copy(k):
        if k < kv_chunks:
            source = w_keyval.at[:, pl.ds(k * TILE, TILE)]
        else:
            source = w_query.at[:, pl.ds((k - kv_chunks) * TILE, TILE)]
        return pltpu.make_async_copy(source, piece(k, d), own_sem.at[k])

    for k in range(chunks):
        own_copy(k).start()

    def token_copy(b):
        part = pl.ds(b * BLOCK, BLOCK)
        return pltpu.make_async_copy(tokens.at[part, :], normed.at[part, :], token_sem.at[b])

    for b in range(blocks):
        token_copy(b).start()
    page_local = pltpu.make_async_copy(outgoing.at[:, d], cache.at[:, d], page_own)
    page_local.start()

    pl.semaphore_wait(barrier, groups + planes - 2)

    def page_copy(s):
        target = rem(d + s, groups)
        return pltpu.make_async_remote_copy(
            src_ref=outgoing.at[:, target],
            dst_ref=cache.at[:, d],
            send_sem=page_send.at[s - 1],
            recv_sem=page_recv.at[s - 1],
            device_id=(target, m),
            device_id_type=MESH,
        )

    ahead = 3
    for k in range(ahead):
        own_copy(k).wait()
        issue(k)
        if k == 0:
            for s in range(1, groups):
                page_copy(s).start()
    for k in range(ahead, chunks):
        own_copy(k).wait()

    odd = rem(m, 2)
    side = div(m, 2)
    upper = rem(y_bit + m, 2)
    plane_to = 2 * upper + side

    def swap_copy():
        return pltpu.make_async_remote_copy(
            src_ref=w_out,
            dst_ref=relay,
            send_sem=move_send.at[0],
            recv_sem=move_recv.at[0],
            device_id=(y_n, m),
            device_id_type=MESH,
        )

    def lift_copy(source):
        return pltpu.make_async_remote_copy(
            src_ref=source,
            dst_ref=wout.at[d],
            send_sem=move_send.at[1],
            recv_sem=move_recv.at[1],
            device_id=(d, plane_to),
            device_id_type=MESH,
        )

    def stay_copy(source):
        return pltpu.make_async_copy(source, wout.at[d], move_recv.at[1])

    @pl.when(odd == 1)
    def _():
        swap_copy().start()

    @pl.when((odd == 0) & (plane_to == m))
    def _():
        stay_copy(w_out).start()

    @pl.when((odd == 0) & (plane_to != m))
    def _():
        lift_copy(w_out).start()

    step_rows = 16

    def normalize(first, count):
        def body(i, carry):
            part = pl.ds(pl.multiple_of(first + i * step_rows, step_rows), step_rows)
            value = normed[part, :].astype(jnp.float32)
            inverse = lax.rsqrt(jnp.mean(value * value, axis=-1, keepdims=True) + norm_eps)
            normed[part, :] = (value * inverse * gain[...]).astype(jnp.bfloat16)
            return carry

        lax.fori_loop(0, count // step_rows, body, 0)

    for b in range(blocks // 2):
        token_copy(b).wait()
        normalize(b * BLOCK, BLOCK)
    forward(0)
    issue(ahead)
    for b in range(blocks // 2, blocks):
        token_copy(b).wait()
        normalize(b * BLOCK, BLOCK)

    @pl.when(odd == 1)
    def _():
        swap_copy().wait_recv()

    @pl.when((odd == 1) & (plane_to == m))
    def _():
        stay_copy(relay).start()

    @pl.when((odd == 1) & (plane_to != m))
    def _():
        lift_copy(relay).start()

    complete(0)
    forward(1)
    issue(ahead + 1)

    def project(first, k):
        columns = pl.ds(pl.multiple_of(k * TILE, TILE), TILE)
        result = jnp.dot(
            normed[first : first + half_rows, :],
            wqkv[:, columns],
            preferred_element_type=jnp.float32,
        )
        return result + bias[:, columns]

    def rotate(x, first):
        part = slice(first, first + half_rows)
        return (x * cosine[part, :] + pltpu.roll(x, HD // 2, 1) * sine[part, :]).astype(
            jnp.bfloat16
        )

    def project_keyval(g):
        for first in (0, half_rows):
            x = project(first, g)
            keys[first : first + half_rows, g * HD : (g + 1) * HD] = rotate(x[:, :HD], first)
            values[first : first + half_rows, g * HD : (g + 1) * HD] = x[:, HD:].astype(
                jnp.bfloat16
            )

    project_keyval(0)
    forward(2)
    issue(ahead + 2)
    complete(1)
    project_keyval(1)
    for s in range(1, groups):
        page_copy(s).wait_recv()
    page_local.wait()

    factor = HD ** (-0.5) * math.log2(math.e)
    cached_len = groups * cache.shape[2]

    def scores(q, k):
        return lax.dot_general(q, k, (((1,), (1,)), ((), ())), preferred_element_type=jnp.float32)

    def attend(first, t):
        x = project(first, kv_chunks + t)
        for j in range(2):
            query[:, j * HD : (j + 1) * HD] = rotate(x[:, j * HD : (j + 1) * HD], first)

        def head(j, carry):
            mine = pl.ds(pl.multiple_of(j * HD, HD), HD)
            group = div(2 * t + j, per_group)
            own = pl.ds(pl.multiple_of(group * HD, HD), HD)
            target = pl.ds(pl.multiple_of(t * TILE + j * HD, HD), HD)
            old_keys = cache[0, :, :, own].reshape(cached_len, HD)
            old_values = cache[1, :, :, own].reshape(cached_len, HD)
            for begin in range(first, first + half_rows, BLOCK):
                q = query[begin - first : begin - first + BLOCK, mine]
                parts = [(scores(q, old_keys) + mask[...], old_values)]
                if begin:
                    parts.append((scores(q, keys[0:begin, own]), values[0:begin, own]))
                diagonal = scores(q, keys[begin : begin + BLOCK, own])
                row_id = lax.broadcasted_iota(jnp.int32, (BLOCK, BLOCK), 0)
                key_id = lax.broadcasted_iota(jnp.int32, (BLOCK, BLOCK), 1)
                diagonal = jnp.where(key_id <= row_id, diagonal, masked_score)
                parts.append((diagonal, values[begin : begin + BLOCK, own]))
                top = functools.reduce(
                    jnp.maximum, [jnp.max(s, axis=-1, keepdims=True) for s, _ in parts]
                )
                total = None
                result = None
                for s, v in parts:
                    raised = jnp.exp2((s - top) * factor)
                    row_sum = jnp.sum(raised, axis=-1, keepdims=True)
                    term = jnp.dot(
                        raised.astype(jnp.bfloat16), v, preferred_element_type=jnp.float32
                    )
                    total = row_sum if total is None else total + row_sum
                    result = term if result is None else result + term
                att[begin : begin + BLOCK, target] = (result / total).astype(jnp.bfloat16)
            return carry

        lax.fori_loop(0, 2, head, 0)

    slot = odd
    primary = 2 - side
    secondary = 3 * side

    def attended_part(i):
        if isinstance(i, int) and i >= tiles:
            return pl.ds(half_rows + (i - tiles) * BLOCK, BLOCK), pl.ds(0, q_width)
        return pl.ds(0, half_rows), pl.ds(pl.multiple_of(i * TILE, TILE), TILE)

    def z_copy(which, i):
        part, columns = attended_part(i)
        return pltpu.make_async_remote_copy(
            src_ref=att.at[part, columns],
            dst_ref=att_in.at[slot, part, columns],
            send_sem=z_send.at[which, i],
            recv_sem=z_recv.at[slot, i],
            device_id=(d, secondary if which else primary),
            device_id_type=MESH,
        )

    def z_keep(i):
        part, columns = attended_part(i)
        return pltpu.make_async_copy(
            att.at[part, columns], att_in.at[slot, part, columns], z_recv.at[slot, i]
        )

    def z_start(i):
        z_copy(0, i).start()

        @pl.when(m != secondary)
        def _():
            z_copy(1, i).start()

        @pl.when(m == secondary)
        def _():
            z_keep(i).start()

    def z_wait(i):
        part, columns = attended_part(i)
        for s in range(2):
            pltpu.make_async_copy(
                att.at[part, columns], att_in.at[s, part, columns], z_recv.at[s, i]
            ).wait()

    def tile_step(t, carry):
        k = t + kv_chunks
        complete(k)
        attend(0, t)
        z_start(t)

        @pl.when(t < tiles - 1)
        def _():
            forward(k + 1)

        @pl.when(t < tiles - 2)
        def _():
            issue_ahead = k + 2

            @pl.when(issue_ahead >= 2 * ahead)
            def _():
                issue(issue_ahead)

        @pl.when(t == tiles - 2)
        def _():
            stay_copy(relay).wait()
            for part in range(out_parts):
                issue(chunks + part)

        attend(half_rows, t)
        return carry

    lax.fori_loop(0, tiles, tile_step, 0)
    for i in range(tiles, tiles + blocks // 2):
        z_start(i)
    for part in range(out_parts):
        forward(chunks + part)
    for part in range(out_parts):
        complete(chunks + part)

    partner = m + 1 - 2 * odd

    def part_copy(b):
        part = pl.ds(b * BLOCK, BLOCK)
        return pltpu.make_async_remote_copy(
            src_ref=normed.at[part, pl.ds(0, q_width)],
            dst_ref=part_in.at[part, :],
            send_sem=part_send.at[b],
            recv_sem=part_recv.at[b],
            device_id=(d, partner),
            device_id_type=MESH,
        )

    def head_partial(b, q, column_block):
        total = None
        for j in range(2):
            order = j + side * 0 + upper_side * (1 - 2 * j)
            index = order * (groups // 2) + column_block * 2 + q
            term = jnp.dot(
                att_in[j, b * BLOCK : (b + 1) * BLOCK, :],
                wout[index],
                preferred_element_type=jnp.float32,
            )
            total = term if total is None else total + term
        return total

    upper_side = div(m, 2)

    def send_partial(b):
        for q in range(2):
            normed[b * BLOCK : (b + 1) * BLOCK, q * out_cols : (q + 1) * out_cols] = head_partial(
                b, q, 1 - odd
            ).astype(jnp.bfloat16)
        part_copy(b).start()

    def out_copy(b):
        part = pl.ds(b * BLOCK, BLOCK)
        return pltpu.make_async_copy(
            normed.at[part, pl.ds(q_width, q_width)], out.at[part, :], out_sem.at[b]
        )

    def finish(b):
        mine = [head_partial(b, q, odd) for q in range(2)]
        part_copy(b).wait_recv()
        for q in range(2):
            columns = slice(q * out_cols, (q + 1) * out_cols)
            normed[
                b * BLOCK : (b + 1) * BLOCK, q_width + q * out_cols : q_width + (q + 1) * out_cols
            ] = (
                mine[q] + part_in[b * BLOCK : (b + 1) * BLOCK, columns].astype(jnp.float32)
            ).astype(jnp.bfloat16)
        out_copy(b).start()

    for i in range(tiles):
        z_wait(i)
    for b in range(blocks // 2):
        send_partial(b)
    for b in range(blocks // 2, blocks):
        z_wait(tiles + b - blocks // 2)
        send_partial(b)
    for b in range(blocks):
        finish(b)

    for k in range(chunks + out_parts):
        for kind in routes:
            hop(kind, k).wait_send()
    for s in range(1, groups):
        page_copy(s).wait_send()

    @pl.when(odd == 1)
    def _():
        swap_copy().wait_send()

    @pl.when(plane_to != m)
    def _():
        lift_copy(w_out).wait_send()

    for i in range(tiles + blocks // 2):
        z_copy(0, i).wait_send()

        @pl.when(m != secondary)
        def _():
            z_copy(1, i).wait_send()

    for b in range(blocks):
        part_copy(b).wait_send()
        out_copy(b).wait()


def fused_layer(tokens, norm_gain, w_query, b_query, keyvalue_weight, b_keyval, w_out, kv_pool,
                page_owner, page_index, prefix_pages, prompt_device):
    groups = lax.axis_size("dp")
    my_group = lax.axis_index("dp")
    rows, features = tokens.shape
    _, q_width = w_query.shape
    width_kv = keyvalue_weight.shape[2]
    kv_local = width_kv // HD
    page_len = kv_pool.shape[2]
    group_ids = jnp.arange(groups, dtype=jnp.int32)

    plan = page_plan(
        kv_pool, page_owner, page_index, prefix_pages, prompt_device, groups, my_group
    )
    outgoing, bias, my_length = plan
    outgoing = outgoing.reshape(2, groups, CAP * page_len, width_kv)
    cosine, sine = rotary_tables(my_length * page_len + jnp.arange(rows, dtype=jnp.int32))

    def interleave(x):
        return jnp.swapaxes(x.reshape(x.shape[0], 2, kv_local, HD), 1, 2).reshape(x.shape[0], -1)

    w_keyval = interleave(keyvalue_weight)
    bias_row = jnp.concatenate([interleave(b_keyval[None])[0], b_query]).astype(jnp.float32)[None]
    gain = norm_gain.astype(jnp.float32)[None]
    any_spec = pl.BlockSpec(memory_space=pl.ANY)
    vmem = pl.BlockSpec(memory_space=pltpu.VMEM)
    tiles = q_width // (2 * HD)
    chunks = tiles + kv_local
    out_parts = 2
    blocks = rows // BLOCK
    sends = tiles + blocks // 2
    dma = pltpu.SemaphoreType.DMA
    bf16 = jnp.bfloat16
    out, _ = pl.pallas_call(
        fused_kernel,
        in_specs=[any_spec] * 5 + [vmem] * 5,
        out_specs=[any_spec, any_spec],
        out_shape=[
            jax.ShapeDtypeStruct((rows, 2 * w_out.shape[1]), bf16),
            jax.ShapeDtypeStruct(w_out.shape, bf16),
        ],
        scratch_shapes=[
            pltpu.VMEM((rows, features), bf16),
            pltpu.VMEM((features, q_width + 2 * width_kv), bf16),
            pltpu.VMEM((groups,) + w_out.shape, bf16),
            pltpu.VMEM((2, groups, CAP * page_len, width_kv), bf16),
            pltpu.VMEM((rows, width_kv), bf16),
            pltpu.VMEM((rows, width_kv), bf16),
            pltpu.VMEM((rows // 2, 2 * HD), bf16),
            pltpu.VMEM((rows, q_width), bf16),
            pltpu.VMEM((2, rows, q_width), bf16),
            pltpu.VMEM((rows, q_width), bf16),
            dma((blocks,)),
            dma((chunks,)),
            dma((7, chunks + out_parts)),
            dma((7, chunks + out_parts)),
            dma((groups - 1,)),
            dma((groups - 1,)),
            dma,
            dma((2, sends)),
            dma((2, sends)),
            dma((blocks,)),
            dma((blocks,)),
            dma((2,)),
            dma((2,)),
            dma((blocks,)),
        ],
        compiler_params=pltpu.CompilerParams(
            collective_id=0, has_side_effects=True, vmem_limit_bytes=67000000
        ),
    )(tokens, w_query, w_keyval, w_out, outgoing, gain, bias_row, bias, cosine, sine)
    return out


def page_plan(kv_pool, page_owner, page_index, prefix_pages, prompt_device, groups, my_group):
    width_kv = kv_pool.shape[3]
    page_len = kv_pool.shape[2]
    max_pages = page_owner.shape[1]
    group_ids = jnp.arange(groups, dtype=jnp.int32)
    slot_prompt = jnp.sum(
        jnp.where(prompt_device[None, :] == group_ids[:, None], group_ids[None, :], 0), axis=1
    )
    owners_all = jnp.take(page_owner, slot_prompt, axis=0)
    index_all = jnp.take(page_index, slot_prompt, axis=0)
    length_all = jnp.take(prefix_pages, slot_prompt, axis=0)
    slot_ids = jnp.arange(max_pages, dtype=jnp.int32)
    places = jnp.arange(CAP, dtype=jnp.int32)
    used = slot_ids[None, :] < length_all[:, None]
    mine = used & (owners_all == my_group)
    rank = jnp.cumsum(mine.astype(jnp.int32), axis=1) - 1
    chosen = mine[:, None, :] & (rank[:, None, :] == places[None, :, None])
    send_index = jnp.sum(jnp.where(chosen, index_all[:, None, :], 0), axis=2)
    outgoing = jnp.take(kv_pool, send_index.reshape(-1), axis=1).reshape(
        2, groups, CAP, page_len, width_kv
    )
    my_owners = jnp.take(owners_all, my_group, axis=0)
    my_length = jnp.take(length_all, my_group, axis=0)
    my_used = slot_ids < my_length
    counts = jnp.sum(
        ((my_owners[None, :] == group_ids[:, None]) & my_used[None, :]).astype(jnp.int32), axis=1
    )
    page_live = (places[None, :] < counts[:, None]).reshape(-1)
    bias = jnp.where(jnp.repeat(page_live, page_len), 0.0, masked_score).astype(jnp.float32)[None]
    return outgoing, bias, my_length


def solution(mesh):
    return jax.shard_map(
        shards,
        mesh=mesh,
        in_specs=(
            P("dp", None),
            P(),
            P("dp", "mp"),
            P("mp"),
            P("dp", None, "mp"),
            P(None, "mp"),
            P("mp", "dp"),
            P(None, "dp", None, "mp"),
            P(),
            P(),
            P(),
            P(),
        ),
        out_specs=P("dp", "mp"),
        check_vma=False,
    )
```

```python
import functools
import math

import jax
import jax.numpy as jnp
from jax import lax
from jax.experimental import pallas as pl
from jax.experimental.pallas import tpu as pltpu
from jax.sharding import PartitionSpec as P


HD = 128
CAP = 2
ROW_PARTS = 2


rope_theta = 1000000.0
norm_eps = 1e-06
masked_score = -1e30


def rms_normed(rows, norm_gain):
    values = rows.astype(jnp.float32)
    inverse = lax.rsqrt(jnp.mean(values * values, axis=-1, keepdims=True) + norm_eps)
    return (values * inverse * norm_gain.astype(jnp.float32)).astype(jnp.bfloat16)


def rotary_tables(positions):
    half_dim = HD // 2
    frequency = rope_theta ** (-jnp.arange(half_dim, dtype=jnp.float32) * 2.0 / HD)
    angles = positions.astype(jnp.float32)[:, None] * frequency[None, :]
    cosine = jnp.cos(angles)
    sine = jnp.sin(angles)
    return (
        jnp.concatenate([cosine, cosine], axis=-1),
        jnp.concatenate([-sine, sine], axis=-1),
    )


def attention_kernel(block, prev_len, *refs):
    q_ref, k_ref, v_ref, cos_ref, sin_ref, bias_ref, kp_ref, vp_ref = refs[:8]
    refs = refs[8:]
    if prev_len:
        k_prev_ref, v_prev_ref = refs[:2]
        refs = refs[2:]
    o_ref, k_out, v_out = refs
    cosine = cos_ref[...]
    sine = sin_ref[...]

    def rotate(x):
        return (x * cosine + pltpu.roll(x, HD // 2, 1) * sine).astype(jnp.bfloat16)

    @pl.when(pl.program_id(0) == 0)
    def _():
        k_out[...] = rotate(k_ref[...])
        v_out[...] = v_ref[...].astype(jnp.bfloat16)

    query = rotate(q_ref[...])
    factor = HD ** (-0.5) * math.log2(math.e)
    rows = query.shape[0]
    ids = lax.broadcasted_iota(jnp.int32, (block, block), 0)
    keys_id = lax.broadcasted_iota(jnp.int32, (block, block), 1)

    def scores(q, k):
        return lax.dot_general(q, k, (((1,), (1,)), ((), ())), preferred_element_type=jnp.float32)

    for begin in range(0, rows, block):
        q = query[begin : begin + block]
        parts = [(scores(q, kp_ref[0]) + bias_ref[...], vp_ref[0])]
        if prev_len:
            parts.append((scores(q, k_prev_ref[...]), v_prev_ref[...]))
        if begin:
            parts.append((scores(q, k_out[0:begin, :]), v_out[0:begin, :]))
        diagonal = scores(q, k_out[begin : begin + block, :])
        diagonal = jnp.where(keys_id <= ids, diagonal, masked_score)
        parts.append((diagonal, v_out[begin : begin + block, :]))
        top = functools.reduce(
            jnp.maximum, [jnp.max(s, axis=-1, keepdims=True) for s, _ in parts]
        )
        total = None
        out = None
        for s, v in parts:
            raised = jnp.exp2((s - top) * factor)
            row_sum = jnp.sum(raised, axis=-1, keepdims=True)
            term = jnp.dot(raised.astype(jnp.bfloat16), v, preferred_element_type=jnp.float32)
            total = row_sum if total is None else total + row_sum
            out = term if out is None else out + term
        o_ref[begin : begin + block, :] = (out / total).astype(jnp.bfloat16)


def attention(group, qkv, cosine, sine, bias, arrived, prev, per_group):
    rows = qkv.shape[0]
    cached_len = arrived.shape[1]
    block = math.gcd(256, rows)
    const = lambda shape, index: pl.BlockSpec(shape, lambda h: index)
    in_specs = [
        pl.BlockSpec((rows, HD), lambda h: (0, h)),
        const((rows, HD), (0, per_group)),
        const((rows, HD), (0, per_group + 1)),
        const((rows, HD), (0, 0)),
        const((rows, HD), (0, 0)),
        const((1, cached_len), (0, 0)),
        const((1, cached_len, HD), (0, 0, group)),
        const((1, cached_len, HD), (1, 0, group)),
    ]
    operands = [qkv, qkv, qkv, cosine, sine, bias, arrived, arrived]
    prev_len = 0
    if prev is not None:
        prev_len = prev[0].shape[0]
        in_specs += [const((prev_len, HD), (0, 0))] * 2
        operands += list(prev)
    keys = cached_len + prev_len + rows
    return pl.pallas_call(
        functools.partial(attention_kernel, block, prev_len),
        grid=(per_group,),
        in_specs=in_specs,
        out_specs=[
            pl.BlockSpec((rows, HD), lambda h: (0, h)),
            const((rows, HD), (0, 0)),
            const((rows, HD), (0, 0)),
        ],
        out_shape=[
            jax.ShapeDtypeStruct((rows, per_group * HD), jnp.bfloat16),
            jax.ShapeDtypeStruct((rows, HD), jnp.bfloat16),
            jax.ShapeDtypeStruct((rows, HD), jnp.bfloat16),
        ],
        compiler_params=pltpu.CompilerParams(
            dimension_semantics=("arbitrary",), vmem_limit_bytes=40 * 1024 * 1024
        ),
        cost_estimate=pl.CostEstimate(
            flops=8 * per_group * rows * keys * HD,
            bytes_accessed=6 * rows * (per_group + 2) * HD,
            transcendentals=per_group * rows * keys,
        ),
    )(*operands)


def exchange(x, axis, split_axis, concat_axis):
    size = lax.axis_size(axis)
    me = lax.axis_index(axis)
    width = x.shape[split_axis] // size
    span = x.shape[concat_axis]
    shape = list(x.shape)
    shape[split_axis] = width
    shape[concat_axis] = span * size
    result = jnp.zeros(shape, x.dtype)
    for s in range(size):
        target = lax.rem(me + s, size)
        source = lax.rem(me - s + size, size)
        piece = lax.dynamic_slice_in_dim(x, target * width, width, split_axis)
        if s:
            piece = lax.ppermute(piece, axis, [(i, (i + s) % size) for i in range(size)])
        result = lax.dynamic_update_slice_in_dim(result, piece, source * span, concat_axis)
    return result


def shards(*arguments):
    kv_local = arguments[4].shape[2] // HD
    if square_mesh() and kv_local == 2:
        return fused_layer(*arguments)
    return layer(*arguments)


def square_mesh():
    return lax.axis_size("dp") == 8 and lax.axis_size("mp") == 4


def layer(
    tokens,
    norm_gain,
    w_query,
    b_query,
    keyvalue_weight,
    b_keyval,
    w_out,
    kv_pool,
    page_owner,
    page_index,
    prefix_pages,
    prompt_device,
):
    groups = lax.axis_size("dp")
    planes = lax.axis_size("mp")
    my_group = lax.axis_index("dp")
    my_plane = lax.axis_index("mp")
    seq_rows = tokens.shape[0]
    width_kv = keyvalue_weight.shape[2]
    kv_local = width_kv // HD
    heads_local = w_query.shape[1] // HD
    per_group = heads_local // kv_local
    page_len = kv_pool.shape[2]
    max_pages = page_owner.shape[1]
    group_ids = jnp.arange(groups, dtype=jnp.int32)

    width_q = per_group * HD
    gathered = []
    biases = []
    for g in range(kv_local):
        piece = jnp.concatenate(
            [
                w_query[:, g * width_q : (g + 1) * width_q],
                keyvalue_weight[:, 0, g * HD : (g + 1) * HD],
                keyvalue_weight[:, 1, g * HD : (g + 1) * HD],
            ],
            axis=1,
        )
        gathered.append(lax.all_gather(piece, "dp", axis=0, tiled=True))
        biases.append(
            jnp.concatenate(
                [
                    b_query[g * width_q : (g + 1) * width_q],
                    b_keyval[0, g * HD : (g + 1) * HD],
                    b_keyval[1, g * HD : (g + 1) * HD],
                ]
            ).astype(jnp.float32)
        )

    slot_prompt = jnp.sum(
        jnp.where(prompt_device[None, :] == group_ids[:, None], group_ids[None, :], 0), axis=1
    )
    owners_all = jnp.take(page_owner, slot_prompt, axis=0)
    index_all = jnp.take(page_index, slot_prompt, axis=0)
    length_all = jnp.take(prefix_pages, slot_prompt, axis=0)
    slot_ids = jnp.arange(max_pages, dtype=jnp.int32)
    places = jnp.arange(CAP, dtype=jnp.int32)
    used = slot_ids[None, :] < length_all[:, None]
    mine = used & (owners_all == my_group)
    rank = jnp.cumsum(mine.astype(jnp.int32), axis=1) - 1
    chosen = mine[:, None, :] & (rank[:, None, :] == places[None, :, None])
    send_index = jnp.sum(jnp.where(chosen, index_all[:, None, :], 0), axis=2)
    outgoing = jnp.take(kv_pool, send_index.reshape(-1), axis=1).reshape(
        2, groups, CAP, page_len, width_kv
    )
    arrived = lax.all_to_all(outgoing, "dp", split_axis=1, concat_axis=1, tiled=True)
    my_owners = jnp.take(owners_all, my_group, axis=0)
    my_length = jnp.take(length_all, my_group, axis=0)
    my_used = slot_ids < my_length
    counts = jnp.sum(
        ((my_owners[None, :] == group_ids[:, None]) & my_used[None, :]).astype(jnp.int32), axis=1
    )
    page_live = (places[None, :] < counts[:, None]).reshape(-1)
    cached_len = page_live.shape[0] * page_len
    arrived = arrived.reshape(2, cached_len, width_kv)
    bias = jnp.where(jnp.repeat(page_live, page_len), 0.0, masked_score).astype(jnp.float32)[None]

    normed = rms_normed(tokens, norm_gain)
    arrived, w_out = lax.optimization_barrier((arrived, w_out))
    out_rows = exchange(w_out, "dp", 0, 1)
    out_rows = exchange(out_rows, "mp", 1, 0)
    out_weight = lax.all_gather(out_rows, "dp", axis=0, tiled=True)
    out_cols = out_weight.shape[1]
    out_weight = out_weight.reshape(groups, planes, -1, out_cols)
    cosine, sine = rotary_tables(
        my_length * page_len + jnp.arange(seq_rows, dtype=jnp.int32)
    )
    part = seq_rows // ROW_PARTS
    held = [[[] for _ in range(ROW_PARTS)] for _ in range(planes)]
    for g in range(kv_local):
        prev = None
        for r in range(ROW_PARTS):
            rows = slice(r * part, (r + 1) * part)
            qkv = (
                jnp.dot(normed[rows], gathered[g], preferred_element_type=jnp.float32)
                + biases[g]
            )
            attended, keys, values = attention(
                g, qkv, cosine[rows], sine[rows], bias, arrived, prev, per_group
            )
            if prev is None:
                prev = (keys, values)
            else:
                prev = (
                    jnp.concatenate([prev[0], keys], axis=0),
                    jnp.concatenate([prev[1], values], axis=0),
                )
            held[0][r].append(attended)
            for s in range(1, planes):
                high = 1 << (s.bit_length() - 1)
                low = s - high
                _, moved, step = ("relay", held[high][r][g], low) if low else ("send", attended, s)
                held[s][r].append(lax.ppermute(moved, "mp", [(i, i ^ step) for i in range(planes)]))
    weights = []
    for s in range(planes):
        source = my_plane ^ s
        rows_of = lax.dynamic_index_in_dim(out_weight, source, axis=1, keepdims=False)
        weights.append(rows_of.reshape(-1, out_cols))
    outputs = []
    for r in range(ROW_PARTS):
        total = None
        for s in range(planes):
            head_partial = None
            for g in range(kv_local):
                term = jnp.dot(
                    held[s][r][g],
                    weights[s][g * width_q : (g + 1) * width_q],
                    preferred_element_type=jnp.float32,
                )
                head_partial = term if head_partial is None else term + head_partial
            head_partial = head_partial.astype(jnp.bfloat16).astype(jnp.float32)
            total = head_partial if total is None else total + head_partial
        outputs.append(total.astype(jnp.bfloat16))
    return jnp.concatenate(outputs, axis=0)


MESH = pl.DeviceIdType.MESH
BLOCK = 256
TILE = 2 * HD
X, Y, FAR, OWN, OX, OY, OFAR = range(7)


def fused_kernel(
    tokens, w_query, w_keyval, w_out, outgoing, gain, bias, mask, cosine, sine,
    out, relay,
    normed, wqkv, wout, cache, keys, values, query, att, att_in, part_in,
    token_sem, own_sem, send_sem, recv_sem, page_send, page_recv, page_own,
    z_send, z_recv, part_send, part_recv, move_send, move_recv, out_sem,
):
    div, rem = lax.div, lax.rem
    groups = lax.axis_size("dp")
    planes = lax.axis_size("mp")
    d = lax.axis_index("dp")
    m = lax.axis_index("mp")
    rows = tokens.shape[0]
    half_rows = rows // 2
    blocks = rows // BLOCK
    depth = w_query.shape[0]
    q_width = w_query.shape[1]
    tiles = q_width // TILE
    kv_chunks = w_keyval.shape[1] // TILE
    per_group = q_width // HD // kv_chunks
    chunks = kv_chunks + tiles
    out_depth, out_cols = w_out.shape
    out_parts = 2
    part_depth = out_depth // out_parts

    core = rem(d, 2)
    x_bit = rem(div(d, 2), 2)
    y_bit = rem(div(d, 4), 2)
    core_n = d + 1 - 2 * core
    x_n = d + 2 - 4 * x_bit
    y_n = d + 4 - 8 * y_bit
    far = x_n + y_n - d
    flip = rem(m + core, 2)
    far_src = x_n + flip * (y_n - x_n)
    far_dst = y_n + flip * (x_n - y_n)

    def piece(k, owner):
        if isinstance(k, int) and k >= chunks:
            return wout.at[owner, pl.ds((k - chunks) * part_depth, part_depth), :]
        return wqkv.at[
            pl.ds(pl.multiple_of(owner * depth, depth), depth),
            pl.ds(pl.multiple_of(k * TILE, TILE), TILE),
        ]

    routes = {
        X: (d, x_n),
        Y: (d, y_n),
        FAR: (far_src, far_dst),
        OWN: (d, core_n),
        OX: (x_n, core_n),
        OY: (y_n, core_n),
        OFAR: (far, core_n),
    }

    def hop(kind, k):
        owner, target = routes[kind]
        region = piece(k, owner)
        return pltpu.make_async_remote_copy(
            src_ref=region,
            dst_ref=region,
            send_sem=send_sem.at[kind, k],
            recv_sem=recv_sem.at[kind, k],
            device_id=(target, m),
            device_id_type=MESH,
        )

    def issue(k):
        for kind in (X, Y, OWN):
            hop(kind, k).start()

    def forward(k):
        hop(X, k).wait_recv()
        hop(Y, k).wait_recv()
        for kind in (FAR, OX, OY):
            hop(kind, k).start()

    def complete(k):
        hop(FAR, k).wait_recv()
        hop(OFAR, k).start()
        for kind in (OWN, OX, OY, OFAR):
            hop(kind, k).wait_recv()

    barrier = pltpu.get_barrier_semaphore()
    for s in range(1, groups):
        pl.semaphore_signal(
            barrier, inc=1, device_id=(rem(d + s, groups), m), device_id_type=MESH
        )
    for s in range(1, planes):
        pl.semaphore_signal(
            barrier, inc=1, device_id=(d, rem(m + s, planes)), device_id_type=MESH
        )

    kv_at = [g + g * per_group * HD // TILE for g in range(kv_chunks)]

    def own_copy(k):
        if k in kv_at:
            source = w_keyval.at[:, pl.ds(kv_at.index(k) * TILE, TILE)]
        else:
            tile = k - sum(at < k for at in kv_at)
            source = w_query.at[:, pl.ds(tile * TILE, TILE)]
        return pltpu.make_async_copy(source, piece(k, d), own_sem.at[k])

    for k in range(chunks):
        own_copy(k).start()

    def token_copy(b):
        part = pl.ds(b * BLOCK, BLOCK)
        return pltpu.make_async_copy(tokens.at[part, :], normed.at[part, :], token_sem.at[b])

    for b in range(blocks):
        token_copy(b).start()
    page_local = pltpu.make_async_copy(outgoing.at[:, d], cache.at[:, d], page_own)
    page_local.start()

    pl.semaphore_wait(barrier, groups + planes - 2)

    def page_copy(s):
        target = rem(d + s, groups)
        return pltpu.make_async_remote_copy(
            src_ref=outgoing.at[:, target],
            dst_ref=cache.at[:, d],
            send_sem=page_send.at[s - 1],
            recv_sem=page_recv.at[s - 1],
            device_id=(target, m),
            device_id_type=MESH,
        )

    odd = rem(m, 2)
    side = div(m, 2)
    plane_to = 2 * rem(y_bit + flip, 2) + side

    def swap_copy():
        return pltpu.make_async_remote_copy(
            src_ref=w_out,
            dst_ref=relay,
            send_sem=move_send.at[0],
            recv_sem=move_recv.at[0],
            device_id=(y_n, m),
            device_id_type=MESH,
        )

    def lift_copy(source):
        return pltpu.make_async_remote_copy(
            src_ref=source,
            dst_ref=wout.at[d],
            send_sem=move_send.at[1],
            recv_sem=move_recv.at[1],
            device_id=(d, plane_to),
            device_id_type=MESH,
        )

    def stay_copy(source):
        return pltpu.make_async_copy(source, wout.at[d], move_recv.at[1])

    @pl.when(flip == 1)
    def _():
        swap_copy().start()

    @pl.when((flip == 0) & (plane_to == m))
    def _():
        stay_copy(w_out).start()

    @pl.when((flip == 0) & (plane_to != m))
    def _():
        lift_copy(w_out).start()

    ahead = 3
    for k in range(ahead):
        own_copy(k).wait()
        issue(k)
        if k == 0:
            for s in range(1, groups):
                page_copy(s).start()
    for k in range(ahead, chunks):
        own_copy(k).wait()

    step_rows = 16

    def normalize(first, count):
        def body(i, carry):
            part = pl.ds(pl.multiple_of(first + i * step_rows, step_rows), step_rows)
            value = normed[part, :].astype(jnp.float32)
            inverse = lax.rsqrt(jnp.mean(value * value, axis=-1, keepdims=True) + norm_eps)
            normed[part, :] = (value * inverse * gain[...]).astype(jnp.bfloat16)
            return carry

        lax.fori_loop(0, count // step_rows, body, 0)

    for b in range(blocks // 2):
        token_copy(b).wait()
        normalize(b * BLOCK, BLOCK)

    @pl.when(flip == 1)
    def _():
        swap_copy().wait_recv()

    @pl.when((flip == 1) & (plane_to == m))
    def _():
        stay_copy(relay).start()

    @pl.when((flip == 1) & (plane_to != m))
    def _():
        lift_copy(relay).start()

    forward(0)
    issue(ahead)
    for b in range(blocks // 2, blocks):
        token_copy(b).wait()
        normalize(b * BLOCK, BLOCK)

    complete(0)
    forward(1)
    issue(ahead + 1)

    def project(first, k):
        columns = pl.ds(pl.multiple_of(k * TILE, TILE), TILE)
        result = jnp.dot(
            normed[first : first + half_rows, :],
            wqkv[:, columns],
            preferred_element_type=jnp.float32,
        )
        return result + bias[:, columns]

    def rotate(x, first):
        part = slice(first, first + half_rows)
        return (x * cosine[part, :] + pltpu.roll(x, HD // 2, 1) * sine[part, :]).astype(
            jnp.bfloat16
        )

    second = kv_at[1] - 1

    def chunk_of(t):
        return t + 1 + div(t + second, 2 * second)

    def project_keyval(g):
        for first in (0, half_rows):
            x = project(first, kv_at[g])
            keys[first : first + half_rows, g * HD : (g + 1) * HD] = rotate(x[:, :HD], first)
            values[first : first + half_rows, g * HD : (g + 1) * HD] = x[:, HD:].astype(
                jnp.bfloat16
            )

    project_keyval(0)
    for s in range(1, groups):
        page_copy(s).wait_recv()
    page_local.wait()

    factor = HD ** (-0.5) * math.log2(math.e)
    cached_len = groups * cache.shape[2]

    def scores(q, k):
        return lax.dot_general(q, k, (((1,), (1,)), ((), ())), preferred_element_type=jnp.float32)

    def attend(first, t):
        x = project(first, chunk_of(t))
        for j in range(2):
            query[:, j * HD : (j + 1) * HD] = rotate(x[:, j * HD : (j + 1) * HD], first)

        def head(j, carry):
            mine = pl.ds(pl.multiple_of(j * HD, HD), HD)
            group = div(2 * t + j, per_group)
            own = pl.ds(pl.multiple_of(group * HD, HD), HD)
            target = pl.ds(pl.multiple_of(t * TILE + j * HD, HD), HD)
            old_keys = cache[0, :, :, own].reshape(cached_len, HD)
            old_values = cache[1, :, :, own].reshape(cached_len, HD)
            for begin in range(first, first + half_rows, BLOCK):
                q = query[begin - first : begin - first + BLOCK, mine]
                parts = [(scores(q, old_keys) + mask[...], old_values)]
                if begin:
                    parts.append((scores(q, keys[0:begin, own]), values[0:begin, own]))
                diagonal = scores(q, keys[begin : begin + BLOCK, own])
                row_id = lax.broadcasted_iota(jnp.int32, (BLOCK, BLOCK), 0)
                key_id = lax.broadcasted_iota(jnp.int32, (BLOCK, BLOCK), 1)
                diagonal = jnp.where(key_id <= row_id, diagonal, masked_score)
                parts.append((diagonal, values[begin : begin + BLOCK, own]))
                top = functools.reduce(
                    jnp.maximum, [jnp.max(s, axis=-1, keepdims=True) for s, _ in parts]
                )
                total = None
                result = None
                for s, v in parts:
                    raised = jnp.exp2((s - top) * factor)
                    row_sum = jnp.sum(raised, axis=-1, keepdims=True)
                    term = jnp.dot(
                        raised.astype(jnp.bfloat16), v, preferred_element_type=jnp.float32
                    )
                    total = row_sum if total is None else total + row_sum
                    result = term if result is None else result + term
                att[begin : begin + BLOCK, target] = (result / total).astype(jnp.bfloat16)
            return carry

        lax.fori_loop(0, 2, head, 0)

    slot = odd
    primary = 2 - side
    secondary = 3 * side

    def attended_part(i):
        if isinstance(i, int) and i >= tiles:
            return pl.ds(half_rows + (i - tiles) * BLOCK, BLOCK), pl.ds(0, q_width)
        return pl.ds(0, half_rows), pl.ds(pl.multiple_of(i * TILE, TILE), TILE)

    def z_copy(which, i):
        part, columns = attended_part(i)
        return pltpu.make_async_remote_copy(
            src_ref=att.at[part, columns],
            dst_ref=att_in.at[slot, part, columns],
            send_sem=z_send.at[which, i],
            recv_sem=z_recv.at[slot, i],
            device_id=(d, secondary if which else primary),
            device_id_type=MESH,
        )

    def z_keep(i):
        part, columns = attended_part(i)
        return pltpu.make_async_copy(
            att.at[part, columns], att_in.at[slot, part, columns], z_recv.at[slot, i]
        )

    def z_start(i):
        z_copy(0, i).start()

        @pl.when(m != secondary)
        def _():
            z_copy(1, i).start()

        @pl.when(m == secondary)
        def _():
            z_keep(i).start()

    def z_wait(i):
        part, columns = attended_part(i)
        for s in range(2):
            pltpu.make_async_copy(
                att.at[part, columns], att_in.at[s, part, columns], z_recv.at[s, i]
            ).wait()

    parts = range(chunks, chunks + out_parts)

    def out_issue(block):
        @pl.when(x_bit == block)
        def _():
            for k in parts:
                issue(k)

    def out_forward(block):
        @pl.when(x_bit == block)
        def _():
            for k in parts:
                hop(Y, k).wait_recv()

                @pl.when(flip == 1)
                def _():
                    hop(FAR, k).start()

                hop(OY, k).start()

        @pl.when(x_bit != block)
        def _():
            for k in parts:
                hop(X, k).wait_recv()

                @pl.when(flip == 0)
                def _():
                    hop(FAR, k).start()

                hop(OX, k).start()

    def out_complete(block):
        @pl.when(x_bit == block)
        def _():
            for k in parts:
                hop(OWN, k).wait_recv()
                hop(OY, k).wait_recv()

        @pl.when(x_bit != block)
        def _():
            for k in parts:
                hop(FAR, k).wait_recv()
                hop(OFAR, k).start()
            for k in parts:
                hop(OX, k).wait_recv()
                hop(OFAR, k).wait_recv()

    def tile_step(t, carry):
        k = chunk_of(t)

        @pl.when(t == second)
        def _():
            forward(kv_at[1] + 1)
            complete(kv_at[1])
            project_keyval(1)

        complete(k)
        attend(0, t)
        z_start(t)

        @pl.when(t < tiles - 1)
        def _():
            forward(k + 1)

        @pl.when(t < chunks - ahead - 2)
        def _():
            issue(k + ahead + 1)

        @pl.when(t == tiles - 2)
        def _():
            stay_copy(relay).wait()
            out_issue(1 - odd)

        attend(half_rows, t)
        return carry

    lax.fori_loop(0, tiles, tile_step, 0)
    for i in range(tiles, tiles + blocks // 2):
        z_start(i)
    out_forward(1 - odd)
    out_issue(odd)
    out_complete(1 - odd)

    partner = m + 1 - 2 * odd

    def part_copy(b):
        part = pl.ds(b * BLOCK, BLOCK)
        return pltpu.make_async_remote_copy(
            src_ref=normed.at[part, pl.ds(0, q_width)],
            dst_ref=part_in.at[part, :],
            send_sem=part_send.at[b],
            recv_sem=part_recv.at[b],
            device_id=(d, partner),
            device_id_type=MESH,
        )

    def head_partial(b, q, column_block):
        total = None
        for j in range(2):
            index = rem(j + side + q, 2) * (groups // 2) + column_block * 2 + q
            term = jnp.dot(
                att_in[j, b * BLOCK : (b + 1) * BLOCK, :],
                wout[index],
                preferred_element_type=jnp.float32,
            )
            total = term if total is None else total + term
        return total

    def send_partial(b):
        for q in range(2):
            normed[b * BLOCK : (b + 1) * BLOCK, q * out_cols : (q + 1) * out_cols] = head_partial(
                b, q, 1 - odd
            ).astype(jnp.bfloat16)
        part_copy(b).start()

    def out_copy(b):
        part = pl.ds(b * BLOCK, BLOCK)
        return pltpu.make_async_copy(
            normed.at[part, pl.ds(q_width, q_width)], out.at[part, :], out_sem.at[b]
        )

    def finish(b):
        mine = [head_partial(b, q, odd) for q in range(2)]
        part_copy(b).wait_recv()
        for q in range(2):
            columns = slice(q * out_cols, (q + 1) * out_cols)
            normed[
                b * BLOCK : (b + 1) * BLOCK, q_width + q * out_cols : q_width + (q + 1) * out_cols
            ] = (
                mine[q] + part_in[b * BLOCK : (b + 1) * BLOCK, columns].astype(jnp.float32)
            ).astype(jnp.bfloat16)
        out_copy(b).start()

    for i in range(tiles):
        z_wait(i)
    for b in range(blocks // 2):
        send_partial(b)
    out_forward(odd)
    out_complete(odd)
    for b in range(blocks // 2, blocks):
        z_wait(tiles + b - blocks // 2)
        send_partial(b)
    for b in range(blocks):
        finish(b)

    for k in range(chunks + out_parts):
        for kind in routes:
            hop(kind, k).wait_send()
    for s in range(1, groups):
        page_copy(s).wait_send()

    @pl.when(flip == 1)
    def _():
        swap_copy().wait_send()

    @pl.when(plane_to != m)
    def _():
        lift_copy(w_out).wait_send()

    for i in range(tiles + blocks // 2):
        z_copy(0, i).wait_send()

        @pl.when(m != secondary)
        def _():
            z_copy(1, i).wait_send()

    for b in range(blocks):
        part_copy(b).wait_send()
        out_copy(b).wait()


def fused_layer(tokens, norm_gain, w_query, b_query, keyvalue_weight, b_keyval, w_out, kv_pool,
                page_owner, page_index, prefix_pages, prompt_device):
    groups = lax.axis_size("dp")
    my_group = lax.axis_index("dp")
    rows, features = tokens.shape
    _, q_width = w_query.shape
    width_kv = keyvalue_weight.shape[2]
    kv_local = width_kv // HD
    page_len = kv_pool.shape[2]
    group_ids = jnp.arange(groups, dtype=jnp.int32)

    plan = page_plan(
        kv_pool, page_owner, page_index, prefix_pages, prompt_device, groups, my_group
    )
    outgoing, bias, my_length = plan
    outgoing = outgoing.reshape(2, groups, CAP * page_len, width_kv)
    cosine, sine = rotary_tables(my_length * page_len + jnp.arange(rows, dtype=jnp.int32))

    def interleave(x):
        return jnp.swapaxes(x.reshape(x.shape[0], 2, kv_local, HD), 1, 2).reshape(x.shape[0], -1)

    w_keyval = interleave(keyvalue_weight)
    b_pair = interleave(b_keyval[None])[0]
    pieces = []
    per_group = q_width // HD // kv_local
    for g in range(kv_local):
        begin, end = ((g + i) * per_group * HD // (2 * HD) * 2 * HD for i in range(2))
        end = q_width if g == kv_local - 1 else end
        pieces += [b_pair[g * 2 * HD : (g + 1) * 2 * HD], b_query[begin:end]]
    bias_row = jnp.concatenate(pieces).astype(jnp.float32)[None]
    gain = norm_gain.astype(jnp.float32)[None]
    any_spec = pl.BlockSpec(memory_space=pl.ANY)
    vmem = pl.BlockSpec(memory_space=pltpu.VMEM)
    tiles = q_width // (2 * HD)
    chunks = tiles + kv_local
    out_parts = 2
    blocks = rows // BLOCK
    sends = tiles + blocks // 2
    dma = pltpu.SemaphoreType.DMA
    bf16 = jnp.bfloat16
    out, _ = pl.pallas_call(
        fused_kernel,
        in_specs=[any_spec] * 5 + [vmem] * 5,
        out_specs=[any_spec, any_spec],
        out_shape=[
            jax.ShapeDtypeStruct((rows, 2 * w_out.shape[1]), bf16),
            jax.ShapeDtypeStruct(w_out.shape, bf16),
        ],
        scratch_shapes=[
            pltpu.VMEM((rows, features), bf16),
            pltpu.VMEM((features, q_width + 2 * width_kv), bf16),
            pltpu.VMEM((groups,) + w_out.shape, bf16),
            pltpu.VMEM((2, groups, CAP * page_len, width_kv), bf16),
            pltpu.VMEM((rows, width_kv), bf16),
            pltpu.VMEM((rows, width_kv), bf16),
            pltpu.VMEM((rows // 2, 2 * HD), bf16),
            pltpu.VMEM((rows, q_width), bf16),
            pltpu.VMEM((2, rows, q_width), bf16),
            pltpu.VMEM((rows, q_width), bf16),
            dma((blocks,)),
            dma((chunks,)),
            dma((7, chunks + out_parts)),
            dma((7, chunks + out_parts)),
            dma((groups - 1,)),
            dma((groups - 1,)),
            dma,
            dma((2, sends)),
            dma((2, sends)),
            dma((blocks,)),
            dma((blocks,)),
            dma((2,)),
            dma((2,)),
            dma((blocks,)),
        ],
        compiler_params=pltpu.CompilerParams(
            collective_id=0, has_side_effects=True, vmem_limit_bytes=67000000
        ),
    )(tokens, w_query, w_keyval, w_out, outgoing, gain, bias_row, bias, cosine, sine)
    return out


def page_plan(kv_pool, page_owner, page_index, prefix_pages, prompt_device, groups, my_group):
    width_kv = kv_pool.shape[3]
    page_len = kv_pool.shape[2]
    max_pages = page_owner.shape[1]
    group_ids = jnp.arange(groups, dtype=jnp.int32)
    chosen_prompt = prompt_device[None, :] == group_ids[:, None]

    def by_slot(table):
        pick = chosen_prompt.reshape(chosen_prompt.shape + (1,) * (table.ndim - 1))
        return jnp.sum(jnp.where(pick, table[None], 0), axis=1)

    def of_mine(table):
        pick = (prompt_device == my_group).reshape((-1,) + (1,) * (table.ndim - 1))
        return jnp.sum(jnp.where(pick, table, 0), axis=0)

    slot_ids = jnp.arange(max_pages, dtype=jnp.int32)
    places = jnp.arange(CAP, dtype=jnp.int32)
    used = slot_ids[None, :] < by_slot(prefix_pages)[:, None]
    mine = used & (by_slot(page_owner) == my_group)
    earlier = slot_ids[None, :] <= slot_ids[:, None]
    rank = jnp.sum((mine[:, None, :] & earlier[None]).astype(jnp.int32), axis=2) - 1
    chosen = mine[:, None, :] & (rank[:, None, :] == places[None, :, None])
    send_index = jnp.sum(jnp.where(chosen, by_slot(page_index)[:, None, :], 0), axis=2)
    outgoing = kv_pool.at[:, send_index.reshape(-1)].get(mode="promise_in_bounds").reshape(
        2, groups, CAP, page_len, width_kv
    )
    my_owners = of_mine(page_owner)
    my_length = of_mine(prefix_pages)
    my_used = slot_ids < my_length
    counts = jnp.sum(
        ((my_owners[None, :] == group_ids[:, None]) & my_used[None, :]).astype(jnp.int32), axis=1
    )
    page_live = (places[None, :] < counts[:, None]).reshape(-1)
    bias = jnp.where(jnp.repeat(page_live, page_len), 0.0, masked_score).astype(jnp.float32)[None]
    return outgoing, bias, my_length


def solution(mesh):
    return jax.shard_map(
        shards,
        mesh=mesh,
        in_specs=(
            P("dp", None),
            P(),
            P("dp", "mp"),
            P("mp"),
            P("dp", None, "mp"),
            P(None, "mp"),
            P("mp", "dp"),
            P(None, "dp", None, "mp"),
            P(),
            P(),
            P(),
            P(),
        ),
        out_specs=P("dp", "mp"),
        check_vma=False,
    )
```

```python
import functools
import math

import jax
import jax.numpy as jnp
from jax import lax
from jax.experimental import pallas as pl
from jax.experimental.pallas import tpu as pltpu
from jax.sharding import PartitionSpec as P


HD = 128
CAP = 2
ROW_PARTS = 2


rope_theta = 1000000.0
norm_eps = 1e-06
masked_score = -1e30


def rms_normed(rows, norm_gain):
    values = rows.astype(jnp.float32)
    inverse = lax.rsqrt(jnp.mean(values * values, axis=-1, keepdims=True) + norm_eps)
    return (values * inverse * norm_gain.astype(jnp.float32)).astype(jnp.bfloat16)


def rotary_tables(positions):
    half_dim = HD // 2
    frequency = rope_theta ** (-jnp.arange(half_dim, dtype=jnp.float32) * 2.0 / HD)
    angles = positions.astype(jnp.float32)[:, None] * frequency[None, :]
    cosine = jnp.cos(angles)
    sine = jnp.sin(angles)
    return (
        jnp.concatenate([cosine, cosine], axis=-1),
        jnp.concatenate([-sine, sine], axis=-1),
    )


def attention_kernel(block, prev_len, *refs):
    q_ref, k_ref, v_ref, cos_ref, sin_ref, bias_ref, kp_ref, vp_ref = refs[:8]
    refs = refs[8:]
    if prev_len:
        k_prev_ref, v_prev_ref = refs[:2]
        refs = refs[2:]
    o_ref, k_out, v_out = refs
    cosine = cos_ref[...]
    sine = sin_ref[...]

    def rotate(x):
        return (x * cosine + pltpu.roll(x, HD // 2, 1) * sine).astype(jnp.bfloat16)

    @pl.when(pl.program_id(0) == 0)
    def _():
        k_out[...] = rotate(k_ref[...])
        v_out[...] = v_ref[...].astype(jnp.bfloat16)

    query = rotate(q_ref[...])
    factor = HD ** (-0.5) * math.log2(math.e)
    rows = query.shape[0]
    ids = lax.broadcasted_iota(jnp.int32, (block, block), 0)
    keys_id = lax.broadcasted_iota(jnp.int32, (block, block), 1)

    def scores(q, k):
        return lax.dot_general(q, k, (((1,), (1,)), ((), ())), preferred_element_type=jnp.float32)

    for begin in range(0, rows, block):
        q = query[begin : begin + block]
        parts = [(scores(q, kp_ref[0]) + bias_ref[...], vp_ref[0])]
        if prev_len:
            parts.append((scores(q, k_prev_ref[...]), v_prev_ref[...]))
        if begin:
            parts.append((scores(q, k_out[0:begin, :]), v_out[0:begin, :]))
        diagonal = scores(q, k_out[begin : begin + block, :])
        diagonal = jnp.where(keys_id <= ids, diagonal, masked_score)
        parts.append((diagonal, v_out[begin : begin + block, :]))
        top = functools.reduce(
            jnp.maximum, [jnp.max(s, axis=-1, keepdims=True) for s, _ in parts]
        )
        total = None
        out = None
        for s, v in parts:
            raised = jnp.exp2((s - top) * factor)
            row_sum = jnp.sum(raised, axis=-1, keepdims=True)
            term = jnp.dot(raised.astype(jnp.bfloat16), v, preferred_element_type=jnp.float32)
            total = row_sum if total is None else total + row_sum
            out = term if out is None else out + term
        o_ref[begin : begin + block, :] = (out / total).astype(jnp.bfloat16)


def attention(group, qkv, cosine, sine, bias, arrived, prev, per_group):
    rows = qkv.shape[0]
    cached_len = arrived.shape[1]
    block = math.gcd(256, rows)
    const = lambda shape, index: pl.BlockSpec(shape, lambda h: index)
    in_specs = [
        pl.BlockSpec((rows, HD), lambda h: (0, h)),
        const((rows, HD), (0, per_group)),
        const((rows, HD), (0, per_group + 1)),
        const((rows, HD), (0, 0)),
        const((rows, HD), (0, 0)),
        const((1, cached_len), (0, 0)),
        const((1, cached_len, HD), (0, 0, group)),
        const((1, cached_len, HD), (1, 0, group)),
    ]
    operands = [qkv, qkv, qkv, cosine, sine, bias, arrived, arrived]
    prev_len = 0
    if prev is not None:
        prev_len = prev[0].shape[0]
        in_specs += [const((prev_len, HD), (0, 0))] * 2
        operands += list(prev)
    keys = cached_len + prev_len + rows
    return pl.pallas_call(
        functools.partial(attention_kernel, block, prev_len),
        grid=(per_group,),
        in_specs=in_specs,
        out_specs=[
            pl.BlockSpec((rows, HD), lambda h: (0, h)),
            const((rows, HD), (0, 0)),
            const((rows, HD), (0, 0)),
        ],
        out_shape=[
            jax.ShapeDtypeStruct((rows, per_group * HD), jnp.bfloat16),
            jax.ShapeDtypeStruct((rows, HD), jnp.bfloat16),
            jax.ShapeDtypeStruct((rows, HD), jnp.bfloat16),
        ],
        compiler_params=pltpu.CompilerParams(
            dimension_semantics=("arbitrary",), vmem_limit_bytes=40 * 1024 * 1024
        ),
        cost_estimate=pl.CostEstimate(
            flops=8 * per_group * rows * keys * HD,
            bytes_accessed=6 * rows * (per_group + 2) * HD,
            transcendentals=per_group * rows * keys,
        ),
    )(*operands)


def exchange(x, axis, split_axis, concat_axis):
    size = lax.axis_size(axis)
    me = lax.axis_index(axis)
    width = x.shape[split_axis] // size
    span = x.shape[concat_axis]
    shape = list(x.shape)
    shape[split_axis] = width
    shape[concat_axis] = span * size
    result = jnp.zeros(shape, x.dtype)
    for s in range(size):
        target = lax.rem(me + s, size)
        source = lax.rem(me - s + size, size)
        piece = lax.dynamic_slice_in_dim(x, target * width, width, split_axis)
        if s:
            piece = lax.ppermute(piece, axis, [(i, (i + s) % size) for i in range(size)])
        result = lax.dynamic_update_slice_in_dim(result, piece, source * span, concat_axis)
    return result


def shards(*arguments):
    kv_local = arguments[4].shape[2] // HD
    if square_mesh() and kv_local == 2:
        return fused_layer(*arguments)
    return layer(*arguments)


def square_mesh():
    return lax.axis_size("dp") == 8 and lax.axis_size("mp") == 4


def layer(
    tokens,
    norm_gain,
    w_query,
    b_query,
    keyvalue_weight,
    b_keyval,
    w_out,
    kv_pool,
    page_owner,
    page_index,
    prefix_pages,
    prompt_device,
):
    groups = lax.axis_size("dp")
    planes = lax.axis_size("mp")
    my_group = lax.axis_index("dp")
    my_plane = lax.axis_index("mp")
    seq_rows = tokens.shape[0]
    width_kv = keyvalue_weight.shape[2]
    kv_local = width_kv // HD
    heads_local = w_query.shape[1] // HD
    per_group = heads_local // kv_local
    page_len = kv_pool.shape[2]
    max_pages = page_owner.shape[1]
    group_ids = jnp.arange(groups, dtype=jnp.int32)

    width_q = per_group * HD
    gathered = []
    biases = []
    for g in range(kv_local):
        piece = jnp.concatenate(
            [
                w_query[:, g * width_q : (g + 1) * width_q],
                keyvalue_weight[:, 0, g * HD : (g + 1) * HD],
                keyvalue_weight[:, 1, g * HD : (g + 1) * HD],
            ],
            axis=1,
        )
        gathered.append(lax.all_gather(piece, "dp", axis=0, tiled=True))
        biases.append(
            jnp.concatenate(
                [
                    b_query[g * width_q : (g + 1) * width_q],
                    b_keyval[0, g * HD : (g + 1) * HD],
                    b_keyval[1, g * HD : (g + 1) * HD],
                ]
            ).astype(jnp.float32)
        )

    slot_prompt = jnp.sum(
        jnp.where(prompt_device[None, :] == group_ids[:, None], group_ids[None, :], 0), axis=1
    )
    owners_all = jnp.take(page_owner, slot_prompt, axis=0)
    index_all = jnp.take(page_index, slot_prompt, axis=0)
    length_all = jnp.take(prefix_pages, slot_prompt, axis=0)
    slot_ids = jnp.arange(max_pages, dtype=jnp.int32)
    places = jnp.arange(CAP, dtype=jnp.int32)
    used = slot_ids[None, :] < length_all[:, None]
    mine = used & (owners_all == my_group)
    rank = jnp.cumsum(mine.astype(jnp.int32), axis=1) - 1
    chosen = mine[:, None, :] & (rank[:, None, :] == places[None, :, None])
    send_index = jnp.sum(jnp.where(chosen, index_all[:, None, :], 0), axis=2)
    outgoing = jnp.take(kv_pool, send_index.reshape(-1), axis=1).reshape(
        2, groups, CAP, page_len, width_kv
    )
    arrived = lax.all_to_all(outgoing, "dp", split_axis=1, concat_axis=1, tiled=True)
    my_owners = jnp.take(owners_all, my_group, axis=0)
    my_length = jnp.take(length_all, my_group, axis=0)
    my_used = slot_ids < my_length
    counts = jnp.sum(
        ((my_owners[None, :] == group_ids[:, None]) & my_used[None, :]).astype(jnp.int32), axis=1
    )
    page_live = (places[None, :] < counts[:, None]).reshape(-1)
    cached_len = page_live.shape[0] * page_len
    arrived = arrived.reshape(2, cached_len, width_kv)
    bias = jnp.where(jnp.repeat(page_live, page_len), 0.0, masked_score).astype(jnp.float32)[None]

    normed = rms_normed(tokens, norm_gain)
    arrived, w_out = lax.optimization_barrier((arrived, w_out))
    out_rows = exchange(w_out, "dp", 0, 1)
    out_rows = exchange(out_rows, "mp", 1, 0)
    out_weight = lax.all_gather(out_rows, "dp", axis=0, tiled=True)
    out_cols = out_weight.shape[1]
    out_weight = out_weight.reshape(groups, planes, -1, out_cols)
    cosine, sine = rotary_tables(
        my_length * page_len + jnp.arange(seq_rows, dtype=jnp.int32)
    )
    part = seq_rows // ROW_PARTS
    held = [[[] for _ in range(ROW_PARTS)] for _ in range(planes)]
    for g in range(kv_local):
        prev = None
        for r in range(ROW_PARTS):
            rows = slice(r * part, (r + 1) * part)
            qkv = (
                jnp.dot(normed[rows], gathered[g], preferred_element_type=jnp.float32)
                + biases[g]
            )
            attended, keys, values = attention(
                g, qkv, cosine[rows], sine[rows], bias, arrived, prev, per_group
            )
            if prev is None:
                prev = (keys, values)
            else:
                prev = (
                    jnp.concatenate([prev[0], keys], axis=0),
                    jnp.concatenate([prev[1], values], axis=0),
                )
            held[0][r].append(attended)
            for s in range(1, planes):
                high = 1 << (s.bit_length() - 1)
                low = s - high
                _, moved, step = ("relay", held[high][r][g], low) if low else ("send", attended, s)
                held[s][r].append(lax.ppermute(moved, "mp", [(i, i ^ step) for i in range(planes)]))
    weights = []
    for s in range(planes):
        source = my_plane ^ s
        rows_of = lax.dynamic_index_in_dim(out_weight, source, axis=1, keepdims=False)
        weights.append(rows_of.reshape(-1, out_cols))
    outputs = []
    for r in range(ROW_PARTS):
        total = None
        for s in range(planes):
            head_partial = None
            for g in range(kv_local):
                term = jnp.dot(
                    held[s][r][g],
                    weights[s][g * width_q : (g + 1) * width_q],
                    preferred_element_type=jnp.float32,
                )
                head_partial = term if head_partial is None else term + head_partial
            head_partial = head_partial.astype(jnp.bfloat16).astype(jnp.float32)
            total = head_partial if total is None else total + head_partial
        outputs.append(total.astype(jnp.bfloat16))
    return jnp.concatenate(outputs, axis=0)


MESH = pl.DeviceIdType.MESH
BLOCK = 256
TILE = 2 * HD
X, Y, FAR, OWN, OX, OY, OFAR = range(7)


def fused_kernel(
    tokens, w_query, w_keyval, w_out, outgoing, gain, bias, mask, cosine, sine,
    out, relay,
    normed, wqkv, wout, cache, keys, values, query, att, att_in, part_in,
    token_sem, own_sem, send_sem, recv_sem, page_send, page_recv, page_own,
    z_send, z_recv, part_send, part_recv, move_send, move_recv, out_sem,
):
    div, rem = lax.div, lax.rem
    groups = lax.axis_size("dp")
    planes = lax.axis_size("mp")
    d = lax.axis_index("dp")
    m = lax.axis_index("mp")
    rows = tokens.shape[0]
    half_rows = rows // 2
    blocks = rows // BLOCK
    depth = w_query.shape[0]
    q_width = w_query.shape[1]
    tiles = q_width // TILE
    kv_chunks = w_keyval.shape[1] // TILE
    per_group = q_width // HD // kv_chunks
    chunks = kv_chunks + tiles
    out_depth, out_cols = w_out.shape
    out_parts = 2
    part_depth = out_depth // out_parts

    core = rem(d, 2)
    x_bit = rem(div(d, 2), 2)
    y_bit = rem(div(d, 4), 2)
    core_n = d + 1 - 2 * core
    x_n = d + 2 - 4 * x_bit
    y_n = d + 4 - 8 * y_bit
    far = x_n + y_n - d
    flip = rem(m + core, 2)
    far_src = x_n + flip * (y_n - x_n)
    far_dst = y_n + flip * (x_n - y_n)

    def piece(k, owner):
        if isinstance(k, int) and k >= chunks:
            return wout.at[owner, pl.ds((k - chunks) * part_depth, part_depth), :]
        return wqkv.at[
            pl.ds(pl.multiple_of(owner * depth, depth), depth),
            pl.ds(pl.multiple_of(k * TILE, TILE), TILE),
        ]

    routes = {
        X: (d, x_n),
        Y: (d, y_n),
        FAR: (far_src, far_dst),
        OWN: (d, core_n),
        OX: (x_n, core_n),
        OY: (y_n, core_n),
        OFAR: (far, core_n),
    }

    def hop(kind, k):
        owner, target = routes[kind]
        region = piece(k, owner)
        return pltpu.make_async_remote_copy(
            src_ref=region,
            dst_ref=region,
            send_sem=send_sem.at[kind, k],
            recv_sem=recv_sem.at[kind, k],
            device_id=(target, m),
            device_id_type=MESH,
        )

    def issue(k):
        for kind in (X, Y, OWN):
            hop(kind, k).start()

    def forward(k):
        hop(X, k).wait_recv()
        hop(Y, k).wait_recv()
        for kind in (FAR, OX, OY):
            hop(kind, k).start()

    def complete(k):
        hop(FAR, k).wait_recv()
        hop(OFAR, k).start()
        for kind in (OWN, OX, OY, OFAR):
            hop(kind, k).wait_recv()

    barrier = pltpu.get_barrier_semaphore()
    for s in range(1, groups):
        pl.semaphore_signal(
            barrier, inc=1, device_id=(rem(d + s, groups), m), device_id_type=MESH
        )
    for s in range(1, planes):
        pl.semaphore_signal(
            barrier, inc=1, device_id=(d, rem(m + s, planes)), device_id_type=MESH
        )

    kv_at = [g + g * per_group * HD // TILE for g in range(kv_chunks)]

    def own_copy(k):
        if k in kv_at:
            source = w_keyval.at[:, pl.ds(kv_at.index(k) * TILE, TILE)]
        else:
            tile = k - sum(at < k for at in kv_at)
            source = w_query.at[:, pl.ds(tile * TILE, TILE)]
        return pltpu.make_async_copy(source, piece(k, d), own_sem.at[k])

    for k in range(chunks):
        own_copy(k).start()

    def token_copy(b):
        part = pl.ds(b * BLOCK, BLOCK)
        return pltpu.make_async_copy(tokens.at[part, :], normed.at[part, :], token_sem.at[b])

    for b in range(blocks):
        token_copy(b).start()
    page_local = pltpu.make_async_copy(outgoing.at[:, d], cache.at[:, d], page_own)
    page_local.start()

    pl.semaphore_wait(barrier, groups + planes - 2)

    def page_copy(s):
        target = rem(d + s, groups)
        return pltpu.make_async_remote_copy(
            src_ref=outgoing.at[:, target],
            dst_ref=cache.at[:, d],
            send_sem=page_send.at[s - 1],
            recv_sem=page_recv.at[s - 1],
            device_id=(target, m),
            device_id_type=MESH,
        )

    odd = rem(m, 2)
    side = div(m, 2)
    plane_to = 2 * rem(y_bit + flip, 2) + side

    def swap_copy():
        return pltpu.make_async_remote_copy(
            src_ref=w_out,
            dst_ref=relay,
            send_sem=move_send.at[0],
            recv_sem=move_recv.at[0],
            device_id=(y_n, m),
            device_id_type=MESH,
        )

    def lift_copy(source):
        return pltpu.make_async_remote_copy(
            src_ref=source,
            dst_ref=wout.at[d],
            send_sem=move_send.at[1],
            recv_sem=move_recv.at[1],
            device_id=(d, plane_to),
            device_id_type=MESH,
        )

    def stay_copy(source):
        return pltpu.make_async_copy(source, wout.at[d], move_recv.at[1])

    @pl.when(flip == 1)
    def _():
        swap_copy().start()

    @pl.when((flip == 0) & (plane_to == m))
    def _():
        stay_copy(w_out).start()

    @pl.when((flip == 0) & (plane_to != m))
    def _():
        lift_copy(w_out).start()

    ahead = 3
    for k in range(ahead):
        own_copy(k).wait()
        issue(k)
        if k == 0:
            for s in range(1, groups):
                page_copy(s).start()
    for k in range(ahead, chunks):
        own_copy(k).wait()

    step_rows = 16

    def normalize(first, count):
        def body(i, carry):
            part = pl.ds(pl.multiple_of(first + i * step_rows, step_rows), step_rows)
            value = normed[part, :].astype(jnp.float32)
            inverse = lax.rsqrt(jnp.mean(value * value, axis=-1, keepdims=True) + norm_eps)
            normed[part, :] = (value * inverse * gain[...]).astype(jnp.bfloat16)
            return carry

        lax.fori_loop(0, count // step_rows, body, 0)

    for b in range(blocks // 2):
        token_copy(b).wait()
        normalize(b * BLOCK, BLOCK)

    @pl.when(flip == 1)
    def _():
        swap_copy().wait_recv()

    @pl.when((flip == 1) & (plane_to == m))
    def _():
        stay_copy(relay).start()

    @pl.when((flip == 1) & (plane_to != m))
    def _():
        lift_copy(relay).start()

    forward(0)
    issue(ahead)
    for b in range(blocks // 2, blocks):
        token_copy(b).wait()
        normalize(b * BLOCK, BLOCK)

    complete(0)
    forward(1)
    issue(ahead + 1)

    def project(first, k):
        columns = pl.ds(pl.multiple_of(k * TILE, TILE), TILE)
        result = jnp.dot(
            normed[first : first + half_rows, :],
            wqkv[:, columns],
            preferred_element_type=jnp.float32,
        )
        return result + bias[:, columns]

    def rotate(x, first):
        part = slice(first, first + half_rows)
        return (x * cosine[part, :] + pltpu.roll(x, HD // 2, 1) * sine[part, :]).astype(
            jnp.bfloat16
        )

    second = kv_at[1] - 1

    def chunk_of(t):
        return t + 1 + div(t + second, 2 * second)

    def project_keyval(g):
        for first in (0, half_rows):
            x = project(first, kv_at[g])
            keys[first : first + half_rows, g * HD : (g + 1) * HD] = rotate(x[:, :HD], first)
            values[first : first + half_rows, g * HD : (g + 1) * HD] = x[:, HD:].astype(
                jnp.bfloat16
            )

    project_keyval(0)
    for s in range(1, groups):
        page_copy(s).wait_recv()
    page_local.wait()

    factor = HD ** (-0.5) * math.log2(math.e)
    cached_len = groups * cache.shape[2]

    def scores(q, k):
        return lax.dot_general(q, k, (((1,), (1,)), ((), ())), preferred_element_type=jnp.float32)

    def attend(first, t):
        x = project(first, chunk_of(t))
        for j in range(2):
            query[:, j * HD : (j + 1) * HD] = rotate(x[:, j * HD : (j + 1) * HD], first)

        def head(j, carry):
            mine = pl.ds(pl.multiple_of(j * HD, HD), HD)
            group = div(2 * t + j, per_group)
            own = pl.ds(pl.multiple_of(group * HD, HD), HD)
            target = pl.ds(pl.multiple_of(t * TILE + j * HD, HD), HD)
            old_keys = cache[0, :, :, own].reshape(cached_len, HD)
            old_values = cache[1, :, :, own].reshape(cached_len, HD)
            for begin in range(first, first + half_rows, BLOCK):
                q = query[begin - first : begin - first + BLOCK, mine]
                parts = [(scores(q, old_keys) + mask[...], old_values)]
                if begin:
                    parts.append((scores(q, keys[0:begin, own]), values[0:begin, own]))
                diagonal = scores(q, keys[begin : begin + BLOCK, own])
                row_id = lax.broadcasted_iota(jnp.int32, (BLOCK, BLOCK), 0)
                key_id = lax.broadcasted_iota(jnp.int32, (BLOCK, BLOCK), 1)
                diagonal = jnp.where(key_id <= row_id, diagonal, masked_score)
                parts.append((diagonal, values[begin : begin + BLOCK, own]))
                top = functools.reduce(
                    jnp.maximum, [jnp.max(s, axis=-1, keepdims=True) for s, _ in parts]
                )
                total = None
                result = None
                for s, v in parts:
                    raised = jnp.exp2((s - top) * factor)
                    row_sum = jnp.sum(raised, axis=-1, keepdims=True)
                    term = jnp.dot(
                        raised.astype(jnp.bfloat16), v, preferred_element_type=jnp.float32
                    )
                    total = row_sum if total is None else total + row_sum
                    result = term if result is None else result + term
                att[begin : begin + BLOCK, target] = (result / total).astype(jnp.bfloat16)
            return carry

        lax.fori_loop(0, 2, head, 0)

    slot = odd
    primary = 2 - side
    secondary = 3 * side

    def attended_part(i):
        if isinstance(i, int) and i >= tiles:
            return pl.ds(half_rows + (i - tiles) * BLOCK, BLOCK), pl.ds(0, q_width)
        return pl.ds(0, half_rows), pl.ds(pl.multiple_of(i * TILE, TILE), TILE)

    def z_copy(which, i):
        part, columns = attended_part(i)
        return pltpu.make_async_remote_copy(
            src_ref=att.at[part, columns],
            dst_ref=att_in.at[slot, part, columns],
            send_sem=z_send.at[which, i],
            recv_sem=z_recv.at[slot, i],
            device_id=(d, secondary if which else primary),
            device_id_type=MESH,
        )

    def z_keep(i):
        part, columns = attended_part(i)
        return pltpu.make_async_copy(
            att.at[part, columns], att_in.at[slot, part, columns], z_recv.at[slot, i]
        )

    def z_start(i):
        z_copy(0, i).start()

        @pl.when(m != secondary)
        def _():
            z_copy(1, i).start()

        @pl.when(m == secondary)
        def _():
            z_keep(i).start()

    def z_wait(i):
        part, columns = attended_part(i)
        for s in range(2):
            pltpu.make_async_copy(
                att.at[part, columns], att_in.at[s, part, columns], z_recv.at[s, i]
            ).wait()

    parts = range(chunks, chunks + out_parts)

    def out_issue(block):
        @pl.when(x_bit == block)
        def _():
            for k in parts:
                issue(k)

    def out_forward(block):
        @pl.when(x_bit == block)
        def _():
            for k in parts:
                hop(Y, k).wait_recv()

                @pl.when(flip == 1)
                def _():
                    hop(FAR, k).start()

                hop(OY, k).start()

        @pl.when(x_bit != block)
        def _():
            for k in parts:
                hop(X, k).wait_recv()

                @pl.when(flip == 0)
                def _():
                    hop(FAR, k).start()

                hop(OX, k).start()

    def out_complete(block):
        @pl.when(x_bit == block)
        def _():
            for k in parts:
                hop(OWN, k).wait_recv()
                hop(OY, k).wait_recv()

        @pl.when(x_bit != block)
        def _():
            for k in parts:
                hop(FAR, k).wait_recv()
                hop(OFAR, k).start()
            for k in parts:
                hop(OX, k).wait_recv()
                hop(OFAR, k).wait_recv()

    def tile_step(t, carry):
        k = chunk_of(t)

        @pl.when(t == second)
        def _():
            forward(kv_at[1] + 1)
            complete(kv_at[1])
            project_keyval(1)

        complete(k)
        attend(0, t)
        z_start(t)

        @pl.when(t < tiles - 1)
        def _():
            forward(k + 1)

        @pl.when(t < chunks - ahead - 2)
        def _():
            issue(k + ahead + 1)

        @pl.when(t == tiles - 2)
        def _():
            stay_copy(relay).wait()
            out_issue(1 - odd)

        attend(half_rows, t)
        return carry

    lax.fori_loop(0, tiles, tile_step, 0)
    for i in range(tiles, tiles + blocks // 2):
        z_start(i)
    out_forward(1 - odd)
    out_issue(odd)
    out_complete(1 - odd)

    partner = m + 1 - 2 * odd

    def part_copy(b):
        part = pl.ds(b * BLOCK, BLOCK)
        return pltpu.make_async_remote_copy(
            src_ref=normed.at[part, pl.ds(0, q_width)],
            dst_ref=part_in.at[part, :],
            send_sem=part_send.at[b],
            recv_sem=part_recv.at[b],
            device_id=(d, partner),
            device_id_type=MESH,
        )

    def head_partial(b, q, column_block):
        total = None
        for j in range(2):
            index = rem(j + side + q, 2) * (groups // 2) + column_block * 2 + q
            term = jnp.dot(
                att_in[j, b * BLOCK : (b + 1) * BLOCK, :],
                wout[index],
                preferred_element_type=jnp.float32,
            )
            total = term if total is None else total + term
        return total

    def send_partial(b):
        for q in range(2):
            normed[b * BLOCK : (b + 1) * BLOCK, q * out_cols : (q + 1) * out_cols] = head_partial(
                b, q, 1 - odd
            ).astype(jnp.bfloat16)
        part_copy(b).start()

    def out_copy(b):
        part = pl.ds(b * BLOCK, BLOCK)
        return pltpu.make_async_copy(
            normed.at[part, pl.ds(q_width, q_width)], out.at[part, :], out_sem.at[b]
        )

    def finish(b):
        mine = [head_partial(b, q, odd) for q in range(2)]
        part_copy(b).wait_recv()
        for q in range(2):
            columns = slice(q * out_cols, (q + 1) * out_cols)
            normed[
                b * BLOCK : (b + 1) * BLOCK, q_width + q * out_cols : q_width + (q + 1) * out_cols
            ] = (
                mine[q] + part_in[b * BLOCK : (b + 1) * BLOCK, columns].astype(jnp.float32)
            ).astype(jnp.bfloat16)
        out_copy(b).start()

    for i in range(tiles):
        z_wait(i)
    for b in range(blocks // 2):
        send_partial(b)
    out_forward(odd)
    for b in range(blocks // 2, blocks):
        if b == blocks - 1:
            out_complete(odd)
        z_wait(tiles + b - blocks // 2)
        send_partial(b)
    for b in range(blocks):
        finish(b)

    for k in range(chunks + out_parts):
        for kind in routes:
            hop(kind, k).wait_send()
    for s in range(1, groups):
        page_copy(s).wait_send()

    @pl.when(flip == 1)
    def _():
        swap_copy().wait_send()

    @pl.when(plane_to != m)
    def _():
        lift_copy(w_out).wait_send()

    for i in range(tiles + blocks // 2):
        z_copy(0, i).wait_send()

        @pl.when(m != secondary)
        def _():
            z_copy(1, i).wait_send()

    for b in range(blocks):
        part_copy(b).wait_send()
        out_copy(b).wait()


def fused_layer(tokens, norm_gain, w_query, b_query, keyvalue_weight, b_keyval, w_out, kv_pool,
                page_owner, page_index, prefix_pages, prompt_device):
    groups = lax.axis_size("dp")
    my_group = lax.axis_index("dp")
    rows, features = tokens.shape
    _, q_width = w_query.shape
    width_kv = keyvalue_weight.shape[2]
    kv_local = width_kv // HD
    page_len = kv_pool.shape[2]
    group_ids = jnp.arange(groups, dtype=jnp.int32)

    plan = page_plan(
        kv_pool, page_owner, page_index, prefix_pages, prompt_device, groups, my_group
    )
    outgoing, bias, my_length = plan
    outgoing = outgoing.reshape(2, groups, CAP * page_len, width_kv)
    cosine, sine = rotary_tables(my_length * page_len + jnp.arange(rows, dtype=jnp.int32))

    def interleave(x):
        return jnp.swapaxes(x.reshape(x.shape[0], 2, kv_local, HD), 1, 2).reshape(x.shape[0], -1)

    w_keyval = interleave(keyvalue_weight)
    b_pair = interleave(b_keyval[None])[0]
    pieces = []
    per_group = q_width // HD // kv_local
    for g in range(kv_local):
        begin, end = ((g + i) * per_group * HD // (2 * HD) * 2 * HD for i in range(2))
        end = q_width if g == kv_local - 1 else end
        pieces += [b_pair[g * 2 * HD : (g + 1) * 2 * HD], b_query[begin:end]]
    bias_row = jnp.concatenate(pieces).astype(jnp.float32)[None]
    gain = norm_gain.astype(jnp.float32)[None]
    any_spec = pl.BlockSpec(memory_space=pl.ANY)
    vmem = pl.BlockSpec(memory_space=pltpu.VMEM)
    tiles = q_width // (2 * HD)
    chunks = tiles + kv_local
    out_parts = 2
    blocks = rows // BLOCK
    sends = tiles + blocks // 2
    dma = pltpu.SemaphoreType.DMA
    bf16 = jnp.bfloat16
    out, _ = pl.pallas_call(
        fused_kernel,
        in_specs=[any_spec] * 5 + [vmem] * 5,
        out_specs=[any_spec, any_spec],
        out_shape=[
            jax.ShapeDtypeStruct((rows, 2 * w_out.shape[1]), bf16),
            jax.ShapeDtypeStruct(w_out.shape, bf16),
        ],
        scratch_shapes=[
            pltpu.VMEM((rows, features), bf16),
            pltpu.VMEM((features, q_width + 2 * width_kv), bf16),
            pltpu.VMEM((groups,) + w_out.shape, bf16),
            pltpu.VMEM((2, groups, CAP * page_len, width_kv), bf16),
            pltpu.VMEM((rows, width_kv), bf16),
            pltpu.VMEM((rows, width_kv), bf16),
            pltpu.VMEM((rows // 2, 2 * HD), bf16),
            pltpu.VMEM((rows, q_width), bf16),
            pltpu.VMEM((2, rows, q_width), bf16),
            pltpu.VMEM((rows, q_width), bf16),
            dma((blocks,)),
            dma((chunks,)),
            dma((7, chunks + out_parts)),
            dma((7, chunks + out_parts)),
            dma((groups - 1,)),
            dma((groups - 1,)),
            dma,
            dma((2, sends)),
            dma((2, sends)),
            dma((blocks,)),
            dma((blocks,)),
            dma((2,)),
            dma((2,)),
            dma((blocks,)),
        ],
        compiler_params=pltpu.CompilerParams(
            collective_id=0, has_side_effects=True, vmem_limit_bytes=67000000
        ),
    )(tokens, w_query, w_keyval, w_out, outgoing, gain, bias_row, bias, cosine, sine)
    return out


def page_plan(kv_pool, page_owner, page_index, prefix_pages, prompt_device, groups, my_group):
    width_kv = kv_pool.shape[3]
    page_len = kv_pool.shape[2]
    max_pages = page_owner.shape[1]
    group_ids = jnp.arange(groups, dtype=jnp.int32)
    chosen_prompt = prompt_device[None, :] == group_ids[:, None]

    def by_slot(table):
        pick = chosen_prompt.reshape(chosen_prompt.shape + (1,) * (table.ndim - 1))
        return jnp.sum(jnp.where(pick, table[None], 0), axis=1)

    def of_mine(table):
        pick = (prompt_device == my_group).reshape((-1,) + (1,) * (table.ndim - 1))
        return jnp.sum(jnp.where(pick, table, 0), axis=0)

    slot_ids = jnp.arange(max_pages, dtype=jnp.int32)
    places = jnp.arange(CAP, dtype=jnp.int32)
    used = slot_ids[None, :] < by_slot(prefix_pages)[:, None]
    mine = used & (by_slot(page_owner) == my_group)
    earlier = slot_ids[None, :] <= slot_ids[:, None]
    rank = jnp.sum((mine[:, None, :] & earlier[None]).astype(jnp.int32), axis=2) - 1
    chosen = mine[:, None, :] & (rank[:, None, :] == places[None, :, None])
    send_index = jnp.sum(jnp.where(chosen, by_slot(page_index)[:, None, :], 0), axis=2)
    outgoing = kv_pool.at[:, send_index.reshape(-1)].get(mode="promise_in_bounds").reshape(
        2, groups, CAP, page_len, width_kv
    )
    my_owners = of_mine(page_owner)
    my_length = of_mine(prefix_pages)
    my_used = slot_ids < my_length
    key_ids = jnp.arange(groups * CAP * page_len, dtype=jnp.int32)
    same = my_owners[None, :] == (key_ids // (CAP * page_len))[:, None]
    count = jnp.sum((same & my_used[None, :]).astype(jnp.int32), axis=1)
    live = (key_ids // page_len) % CAP < count
    bias = jnp.where(live, 0.0, masked_score).astype(jnp.float32)[None]
    return outgoing, bias, my_length


def solution(mesh):
    return jax.shard_map(
        shards,
        mesh=mesh,
        in_specs=(
            P("dp", None),
            P(),
            P("dp", "mp"),
            P("mp"),
            P("dp", None, "mp"),
            P(None, "mp"),
            P("mp", "dp"),
            P(None, "dp", None, "mp"),
            P(),
            P(),
            P(),
            P(),
        ),
        out_specs=P("dp", "mp"),
        check_vma=False,
    )
```
